1024 devices in a mesh: expert: 128 (over x, y, core), hidden: 8 (over z).
Axes of the slice: x: 8, y: 8, z: 8, core: 2. Of those that a mesh axis runs over, the one named last changes fastest.
Arguments:
- weight: bfloat16 [128, 1536, 4096], P('expert', 'hidden'), may hold values from -0.15625 to 0.15625
- scales: float32 [128, 12, 32], P('expert'), may hold values from 0.5 to 2
- act_own: bfloat16 [128, 128, 1536], P('expert', None, 'hidden'), may hold values from -6 to 6
- dy_own: bfloat16 [128, 128, 4096], P('expert'), may hold values from -6 to 6
- own_count: int32 [128], P('expert'), may hold values from 1 to 128, as said below
- act_help: bfloat16 [128, 32, 1536], P('expert', None, 'hidden'), may hold values from -6 to 6
- dy_help: bfloat16 [128, 32, 4096], P('expert'), may hold values from -24 to 24
- help_count: int32 [128], P('expert'), may hold values from 1 to 32, as said below
- hot: int32 [1], replicated, may hold values from 0 to 127
Outputs:
- y_own: bfloat16 [128, 128, 4096], P('expert', None, 'hidden')
- dact_own: bfloat16 [128, 128, 1536], P('expert', None, 'hidden')
- own_grad: bfloat16 [128, 1536, 4096], P('expert', 'hidden')
- y_help: bfloat16 [128, 32, 4096], P('expert', None, 'hidden')
- dact_help: bfloat16 [128, 32, 1536], P('expert', None, 'hidden')
- hot_grad: float32 [1536, 4096], P('hidden', 'expert')
The draws below stay inside these ranges and needn't reach their ends.
Inputs may be any that keep to these rules, and one draw needn't show every extreme that they name: `own_count`: some expert has exactly 128 live rows. `help_count`: some group has exactly 32 live rows.
All inputs are finite; a program needn't handle non-finite values.
Results may differ from the reference program's by a relative error of at most 0.013.
Values may be sent and summed in bfloat16 or wider, within the bound.
A program may use at most 32 MiB of HBM per device.

```python
import math
import jax
import jax.numpy as jnp
from jax import lax

D = 4096
FF = 1536
ROWS = 128
HROWS = 32
EXPERTS = 128
GROUPS = 128
N_HIDDEN = 8


def draw_own_count(key, part):
    first = jax.random.fold_in(key, 11)
    second = jax.random.fold_in(key, 12)
    counts = jax.random.randint(first, (EXPERTS,), 1, ROWS + 1, dtype=jnp.int32)
    chosen = jax.random.randint(second, (), 0, EXPERTS, dtype=jnp.int32)
    return counts.at[chosen].set(ROWS)


def draw_help_count(key, part):
    first = jax.random.fold_in(key, 21)
    second = jax.random.fold_in(key, 22)
    counts = jax.random.randint(first, (GROUPS,), 1, HROWS + 1, dtype=jnp.int32)
    chosen = jax.random.randint(second, (), 0, GROUPS, dtype=jnp.int32)
    return counts.at[chosen].set(HROWS)


def raised(array, key, source, target, blocks, factor):
    owner, partner = [(jnp.arange(array.shape[dim]) // (array.shape[dim] // blocks)).reshape([-1 if axis == dim else 1 for axis in range(array.ndim)]) for dim in (source, target)]
    chosen = jax.random.permutation(key, blocks)[partner]
    strong = (owner == chosen) | (owner == (partner + blocks // 2) % blocks)
    return jnp.where(strong, factor * array, array)


def block_levels(key, dims, cuts, least, high):
    gain = 1.0
    for axis_at, parts in cuts:
        heights = jax.random.uniform(jax.random.fold_in(jax.random.fold_in(key, 6), axis_at), (parts,), jnp.float32, least / len(cuts), high / len(cuts))
        gain = gain * jnp.repeat(jnp.exp(heights), dims[axis_at] // parts).reshape((-1,) + (1,) * (len(dims) - 1 - axis_at))
    return gain


def noise(key, dims, spread, limit, split=(), kind=jnp.bfloat16):
    values = jax.random.normal(key, dims, jnp.float32) * spread
    if len(split) > 0:
        values = block_levels(key, dims, split, -0.22, 0.18) * values
    return jnp.clip(values, min=-limit, max=limit).astype(kind)


def noise_with(rng, shape, scale, most, cuts, heavy, held_as=jnp.bfloat16):
    result = scale * jax.random.normal(rng, shape, jnp.float32)
    if cuts:
        result = result * block_levels(rng, shape, cuts, -0.22, 0.18)
    return jnp.clip(raised(result, jax.random.fold_in(rng, 3), *heavy), -most, most).astype(held_as)


def setup_inputs(seed: int = 0) -> dict:
    splits = jax.random.split(jax.random.key(seed), 10)
    return {
        "weight": noise(splits[0], (EXPERTS, FF, D), FF ** -0.5, 0.15625, ((0, 128), (1, 8))),
        "scales": jnp.clip(jnp.exp(math.log(2.0) - 1.3862944 * jax.random.uniform(splits[1], (EXPERTS, FF // 128, D // 128), jnp.float32) ** block_levels(splits[1], (EXPERTS, FF // 128, D // 128), ((0, 128),), -0.2, 0.2)), 0.5, 2.0),
        "act_own": noise(splits[2], (EXPERTS, ROWS, FF), 1.0, 6.0, ((0, 128), (2, 8))),
        "dy_own": noise(splits[3], (EXPERTS, ROWS, D), 1.0, 6.0, ((0, 128),)),
        "own_count": draw_own_count(jax.random.fold_in(splits[9], 71), 0),
        "act_help": noise(splits[5], (GROUPS, HROWS, FF), 1.0, 6.0, ((0, 128), (2, 8))),
        "dy_help": noise_with(splits[6], (GROUPS, HROWS, D), 1.0, 24.0, ((0, 128),), (0, 2, 128, 5.5)),
        "help_count": draw_help_count(jax.random.fold_in(splits[9], 71), 0),
        "hot": jax.random.randint(splits[8], (1,), 0, EXPERTS).astype(jnp.int32),
    }


def dequant(weight, scales):
    full = jnp.repeat(jnp.repeat(scales, 128, axis=0), 128, axis=1)
    return (weight.astype(jnp.float32) * full).astype(jnp.bfloat16)


def masked(values, count):
    live = jnp.arange(values.shape[0], dtype=jnp.int32)[:, None] < count
    return jnp.where(live, values, jnp.zeros_like(values))


def forward_back(weight_deq, rows, grads):
    nrows = rows.shape[0]
    wide = weight_deq.astype(jnp.float32)
    pieces = rows.astype(jnp.float32).reshape(nrows, N_HIDDEN, FF // N_HIDDEN)
    slices = wide.reshape(N_HIDDEN, FF // N_HIDDEN, D)
    partial_value = jnp.einsum("rhf,hfd->hrd", pieces, slices).astype(jnp.bfloat16)
    partial_value = lax.optimization_barrier(partial_value)
    outputs = jnp.sum(partial_value.astype(jnp.float32), axis=0).astype(jnp.bfloat16)
    grads_wide = grads.astype(jnp.float32)
    dact = jnp.einsum("rd,fd->rf", grads_wide, wide).astype(jnp.bfloat16)
    gradient = jnp.einsum("rf,rd->fd", rows.astype(jnp.float32), grads_wide)
    return outputs, dact, gradient


def reference(weight, scales, act_own, dy_own, own_count, act_help, dy_help, help_count, hot):
    def own_expert(items):
        raw, block_scales, rows, grads, count = items
        weight_deq = dequant(raw, block_scales)
        outputs, dact, gradient = forward_back(weight_deq, masked(rows, count), masked(grads, count))
        return outputs, dact, gradient.astype(jnp.bfloat16)

    y_own, dact_own, own_grad = lax.map(own_expert, (weight, scales, act_own, dy_own, own_count))
    hot_index = hot[0].astype(jnp.int32)
    hot_raw = lax.dynamic_index_in_dim(weight, hot_index, 0, keepdims=False)
    hot_scales = lax.dynamic_index_in_dim(scales, hot_index, 0, keepdims=False)
    hot_weight = dequant(hot_raw, hot_scales)

    def one_group(total, items):
        rows, grads, count = items
        outputs, dact, gradient = forward_back(hot_weight, masked(rows, count), masked(grads, count))
        return total + gradient, (outputs, dact)

    start_total = jnp.zeros((FF, D), jnp.float32)
    hot_grad, (y_help, dact_help) = lax.scan(one_group, start_total, (act_help, dy_help, help_count))
    return y_own, dact_own, own_grad, y_help, dact_help, hot_grad
```

```python
import functools

import jax
import jax.numpy as jnp
from jax import lax
from jax.experimental import pallas as pl
from jax.experimental.pallas import tpu as pltpu
from jax.sharding import PartitionSpec as P

MESH = pl.DeviceIdType.MESH
BF16 = jnp.bfloat16
F32 = jnp.float32
LANES = 128
NT = (((1,), (1,)), ((), ()))
TN = (((0,), (0,)), ((), ()))


def kernel(
    cfg,
    hot, own_count, help_count, scales, act_own, act_help, weight, dy_own, dy_help,
    y_own, dact_own, own_grad, y_help, dact_help, hot_grad,
    w_v, dyo_v, deq, own_a, pairs_a, pairs_g, mine, give, got, r1, s2, r2, wf,
    yp, ry, og, gd, ad, dw, rd, ys, ryh, da_give, da_got,
    load_sem, ex_s, ex_r, pair_s, pair_r, xa_s, xa_r, xg_s, xg_r, z_s, z_r,
    s1_s, s1_r, s2_s, s2_r, s3_s, s3_r, s4_s, s4_r, dw_s, dw_r, yh_s, yh_r, da_s, da_r,
):
    n, nz, ff, rows, hrows, depth = cfg
    half = depth // 2
    zblock = depth // nz
    xblock = depth // n
    cols = xblock // (2 * n)
    chunk = 2 * ff // n
    per = ff // chunk
    e, z = lax.axis_index("expert"), lax.axis_index("hidden")
    x, y, c = lax.div(e, 2 * n), lax.rem(lax.div(e, 2), n), lax.rem(e, 2)
    o = 1 - c

    def at(px, py, pc, pz):
        return ((px * n + py) * 2 + pc, pz)

    first = o * x + c * y
    second = o * y + c * x
    first_p = o * y + c * x

    def along_first(p):
        return at(o * p + c * x, o * y + c * p, c, z)

    def along_second(p):
        return at(o * x + c * p, o * p + c * y, c, z)

    def along_x(p):
        return at(p, y, c, z)

    partner = at(x, y, o, z)

    def loop(low, high, body):
        def step(i, carry):
            body(i)
            return carry

        lax.fori_loop(low, high, step, 0)

    def nth(i, count):
        turn = jnp.where(lax.rem(i, 2) == 0, lax.div(i, 2) + 1, count - lax.div(i + 1, 2))
        return jnp.where(i == count - 1, 0, turn)

    def remote(src, dst, send, recv, device):
        return pltpu.make_async_remote_copy(
            src_ref=src, dst_ref=dst, send_sem=send, recv_sem=recv,
            device_id=device, device_id_type=MESH,
        )

    col_p = pl.multiple_of(o * half, half)
    col_m = pl.multiple_of(c * half, half)
    load_wp = pltpu.make_async_copy(
        weight.at[:, pl.ds(col_p, half)], w_v.at[:, pl.ds(col_p, half)], load_sem.at[0]
    )
    load_wm = pltpu.make_async_copy(
        weight.at[:, pl.ds(col_m, half)], w_v.at[:, pl.ds(col_m, half)], load_sem.at[1]
    )
    load_g = pltpu.make_async_copy(
        dy_help.at[:, pl.ds(col_m, half)], pairs_g.at[pl.ds(0, hrows)], load_sem.at[2]
    )
    load_gd = pltpu.make_async_copy(
        dy_help.at[:, pl.ds(pl.multiple_of(x * xblock, xblock), xblock)], gd.at[x], load_sem.at[3]
    )
    load_dyo = pltpu.make_async_copy(dy_own, dyo_v, load_sem.at[4])
    for load in (load_wp, load_wm, load_gd, load_g, load_dyo):
        load.start()

    barrier = pltpu.get_barrier_semaphore()

    def greet(device):
        pl.semaphore_signal(barrier, inc=1, device_id=device, device_id_type=MESH)

    def greet_plane(d):
        px, py = lax.rem(x + d, n), lax.rem(y + d, n)
        greet(at(px, y, c, z))
        greet(at(x, py, c, z))
        greet(at(x, py, o, z))

    def greet_line(d):
        pz = lax.rem(z + d, nz)
        greet(at(x, y, c, pz))
        greet(at(x, y, o, pz))

    greet(partner)
    loop(1, n, greet_plane)
    loop(1, nz, greet_line)

    live_help = lax.broadcasted_iota(jnp.int32, (hrows, ff), 0) < help_count[0]
    live_own = lax.broadcasted_iota(jnp.int32, (rows, ff), 0) < own_count[0]
    help_a = jnp.where(live_help, act_help[...].astype(F32), 0.0).astype(BF16)
    own_a[...] = jnp.where(live_own, act_own[...].astype(F32), 0.0).astype(BF16)
    pairs_a[pl.ds(0, hrows), :] = help_a
    ad[x] = help_a

    flag = jnp.where(hot[0] == e, 1.0, 0.0).astype(F32)

    def scaled(col_base, at_first, dest, i):
        t = lax.rem(at_first + nth(i, n), n)
        for k in range(2):
            tile = lax.div(col_base, LANES) + 2 * t + k
            col = pl.multiple_of(tile * LANES, LANES)
            for part in range(3):
                third = ff // 3
                span = pl.ds(part * third, third)
                scale = scales[lax.div(3 * z + part, 2), tile]
                wide = w_v[span, pl.ds(col, LANES)].astype(F32) * scale
                deq[span, pl.ds(col, LANES)] = wide.astype(BF16)
                dest[2 * i + k, span, :] = (wide * flag).astype(BF16)

    groups = min(4, n)
    each = n // groups

    pl.semaphore_wait(barrier, 3 * (n - 1) + 2 * (nz - 1) + 1)

    def send_x(d):
        p = lax.rem(x + d, n)
        block = pl.ds(pl.multiple_of(p * xblock, xblock), xblock)
        remote(dy_help.at[:, block], gd.at[x], xg_s.at[p], xg_r.at[x], along_x(p)).start()
        remote(
            pairs_a.at[pl.ds(0, hrows)], ad.at[x], xa_s.at[p], xa_r.at[x], along_x(p)
        ).start()

    pair_g = remote(
        dy_help.at[:, pl.ds(col_p, half)], pairs_g.at[pl.ds(hrows, hrows)],
        pair_s.at[0], pair_r.at[0], partner,
    )
    pair_a = remote(
        pairs_a.at[pl.ds(0, hrows)], pairs_a.at[pl.ds(hrows, hrows)],
        pair_s.at[1], pair_r.at[1], partner,
    )
    pair_a.start()

    load_wp.wait()

    def exchange(q):
        tiles = pl.ds(q * 2 * each, 2 * each)
        return remote(give.at[tiles], got.at[tiles], ex_s.at[q], ex_r.at[q], partner)

    def give_group(q):
        for j in range(each):
            scaled(col_p, first_p, give, q * each + j)
        exchange(q).start()

    loop(0, groups, give_group)
    loop(1, n, send_x)
    pair_g.start()
    load_wm.wait()
    loop(0, n, functools.partial(scaled, col_m, first, mine))

    def send_first(i):
        t = lax.rem(first + nth(i, n), n)
        tiles = pl.ds(2 * i, 2)
        mine[tiles] = mine[tiles] + got[tiles]
        remote(mine.at[tiles], r1.at[first], s1_s.at[t], s1_r.at[first], along_first(t)).start()

    def own_partial(pz):
        block = pl.ds(pl.multiple_of(pz * zblock, zblock), zblock)
        return jnp.dot(own_a[...], deq[:, block], preferred_element_type=F32).astype(BF16)

    def send_z(i):
        pz = lax.rem(z + nth(i, nz), nz)
        yp[pz] = own_partial(pz)
        remote(yp.at[pz], ry.at[z], z_s.at[pz], z_r.at[z], at(x, y, c, pz)).start()

    loop(0, nz - 1, send_z)
    ry[z] = own_partial(z)

    for q in range(groups):
        exchange(q).wait_recv()
        for j in range(each):
            i = q * each + j
            if i < n - 1:
                send_first(i)
            else:
                tiles = pl.ds(2 * i, 2)
                r1[first] = mine[tiles] + got[tiles]

    load_dyo.wait()
    kblock = 512

    def dact_step(j, total):
        block = pl.ds(pl.multiple_of(j * kblock, kblock), kblock)
        return total + lax.dot_general(
            dyo_v[:, block], deq[:, block], NT, preferred_element_type=F32
        )

    total = lax.fori_loop(0, depth // kblock, dact_step, jnp.zeros((rows, ff), F32))
    dact_own[...] = jnp.where(live_own, total, 0.0).astype(BF16)

    def grad_step(j):
        block = pl.ds(pl.multiple_of(j * kblock, kblock), kblock)
        og[:, block] = lax.dot_general(
            own_a[...], dyo_v[:, block], TN, preferred_element_type=F32
        ).astype(BF16)

    loop(0, depth // kblock, grad_step)
    store_og = pltpu.make_async_copy(og, own_grad, load_sem.at[5])
    store_og.start()

    load_gd.wait()

    def wait_x(d):
        p = lax.rem(x + d, n)
        remote(gd.at[p], gd.at[p], xg_s.at[p], xg_r.at[p], along_x(p)).wait_recv()
        remote(ad.at[p], ad.at[p], xa_s.at[p], xa_r.at[p], along_x(p)).wait_recv()

    loop(1, n, wait_x)
    dw[...] = lax.dot_general(
        gd[...].reshape(n * hrows, xblock), ad[...].reshape(n * hrows, ff), TN,
        preferred_element_type=F32,
    )

    def wait_first(d):
        p = lax.rem(first + d, n)
        remote(r1.at[p], r1.at[p], s1_s.at[p], s1_r.at[p], along_first(p)).wait_recv()

    loop(1, n, wait_first)

    def sum_first(i):
        k, span = lax.rem(i, 2), pl.ds(pl.multiple_of(lax.div(i, 2) * chunk, chunk), chunk)
        piece = r1[0, k, span, :].astype(F32)
        for p in range(1, n):
            piece = piece + r1[p, k, span, :].astype(F32)
        s2[k, span, :] = piece.astype(BF16)

    loop(0, 2 * per, sum_first)

    def place(p):
        return lax.div(p, per), pl.ds(pl.multiple_of(lax.rem(p, per) * chunk, chunk), chunk)

    def send_second(i):
        p = lax.rem(second + nth(i, n), n)
        k, span = place(p)
        remote(
            s2.at[k, span], r2.at[second], s2_s.at[p], s2_r.at[second], along_second(p)
        ).start()

    loop(0, n - 1, send_second)
    my_k, my_span = place(second)
    r2[second] = s2[my_k, my_span, :]

    def wait_second(d):
        p = lax.rem(second + d, n)
        remote(r2.at[p], r2.at[p], s2_s.at[p], s2_r.at[p], along_second(p)).wait_recv()

    loop(1, n, wait_second)
    piece = r2[0].astype(F32)
    for p in range(1, n):
        piece = piece + r2[p].astype(F32)
    spot = wf.at[2 * first + my_k, my_span]
    spot[...] = piece.astype(BF16)

    def send_third(i):
        p = lax.rem(second + nth(i, n), n)
        remote(spot, spot, s3_s.at[p], s3_r.at[second], along_second(p)).start()

    loop(0, n - 1, send_third)

    def send_dw(i):
        p = lax.rem(y + nth(i, n), n)
        for pc in range(2):
            part = pl.ds(pl.multiple_of((2 * p + pc) * cols, cols), cols)
            remote(
                dw.at[part], rd.at[2 * y + c], dw_s.at[2 * p + pc], dw_r.at[2 * y + c],
                at(x, p, pc, z),
            ).start()

    loop(0, n - 1, send_dw)
    mine_part = pl.ds(pl.multiple_of((2 * y + c) * cols, cols), cols)
    other_part = pl.ds(pl.multiple_of((2 * y + o) * cols, cols), cols)
    dw_pair = remote(
        dw.at[other_part], rd.at[2 * y + c], dw_s.at[2 * y + o], dw_r.at[2 * y + c], partner
    )
    dw_pair.start()
    rd[2 * y + c] = dw[mine_part, :]

    def wait_third(d):
        p = lax.rem(second + d, n)
        k, span = place(p)
        there = wf.at[2 * first + k, span]
        remote(there, there, s3_s.at[p], s3_r.at[p], along_second(p)).wait_recv()

    loop(1, n, wait_third)

    whole = wf.at[pl.ds(2 * first, 2)]

    def send_fourth(i):
        p = lax.rem(first + nth(i, n), n)
        remote(whole, whole, s4_s.at[p], s4_r.at[first], along_first(p)).start()

    loop(0, n - 1, send_fourth)

    def wait_z(d):
        p = lax.rem(z + d, nz)
        remote(ry.at[p], ry.at[p], z_s.at[p], z_r.at[p], at(x, y, c, p)).wait_recv()

    loop(1, nz, wait_z)

    def sum_z(i):
        span = pl.ds(pl.multiple_of(i * 16, 16), 16)
        piece = ry[0, span, :].astype(F32)
        for p in range(1, nz):
            piece = piece + ry[p, span, :].astype(F32)
        y_own[span, :] = piece.astype(BF16)

    loop(0, rows // 16, sum_z)

    def wait_dw(d):
        p = lax.rem(y + d, n)
        for pc in range(2):
            slot = 2 * p + pc
            remote(
                rd.at[slot], rd.at[slot], dw_s.at[slot], dw_r.at[slot], at(x, p, pc, z)
            ).wait_recv()

    loop(1, n, wait_dw)
    remote(
        rd.at[2 * y + o], rd.at[2 * y + o], dw_s.at[2 * y + o], dw_r.at[2 * y + o], partner
    ).wait_recv()
    total = rd[0]
    for p in range(1, 2 * n):
        total = total + rd[p]
    hot_grad[...] = total.T

    load_g.wait()
    pair_g.wait_recv()
    pair_a.wait_recv()
    blocks = half // zblock
    tiles_per = zblock // LANES

    def wait_fourth(p):
        there = wf.at[pl.ds(2 * p, 2)]
        remote(there, there, s4_s.at[p], s4_r.at[p], along_first(p)).wait_recv()

    da = jnp.zeros((2 * hrows, ff), F32)
    for m in range(blocks):
        pz = c * blocks + m
        for p in range(m * tiles_per // 2, (m + 1) * tiles_per // 2):
            pl.when(first != p)(functools.partial(wait_fourth, p))
        block = jnp.concatenate([wf[m * tiles_per + j] for j in range(tiles_per)], axis=1)
        out = jnp.dot(pairs_a[...], block, preferred_element_type=F32).astype(BF16)
        ys[m] = out.reshape(2, hrows, zblock)
        remote(
            ys.at[m, 1], ryh.at[z], yh_s.at[2 * m + 1], yh_r.at[z], at(x, y, o, pz)
        ).start()

        @pl.when(pz != z)
        def _():
            remote(
                ys.at[m, 0], ryh.at[z], yh_s.at[2 * m], yh_r.at[z], at(x, y, c, pz)
            ).start()

        @pl.when(pz == z)
        def _():
            ryh[z] = ys[m, 0]

        da = da + lax.dot_general(
            pairs_g[:, m * zblock : (m + 1) * zblock], block, NT, preferred_element_type=F32
        )
    da_give[...] = da[hrows:]
    da_copy = remote(da_give, da_got, da_s.at[0], da_r.at[0], partner)
    da_copy.start()

    source = lax.div(z, blocks)

    def wait_yh(p):
        @pl.when((p != z) | (source != c))
        def _():
            remote(
                ryh.at[p], ryh.at[p], yh_s.at[0], yh_r.at[p], at(x, y, source, p)
            ).wait_recv()

    da_copy.wait_recv()
    dact_help[...] = jnp.where(live_help, da[:hrows] + da_got[...], 0.0).astype(BF16)

    loop(0, nz, wait_yh)
    piece = ryh[0].astype(F32)
    for p in range(1, nz):
        piece = piece + ryh[p].astype(F32)
    y_help[...] = piece.astype(BF16)

    store_og.wait()
    pair_a.wait_send()
    pair_g.wait_send()
    dw_pair.wait_send()
    da_copy.wait_send()

    def drain_exchange(q):
        exchange(q).wait_send()

    loop(0, groups, drain_exchange)

    def drain_plane(d):
        px, pf, ps, py = (lax.rem(v + d, n) for v in (x, first, second, y))
        remote(gd.at[px], gd.at[px], xg_s.at[px], xg_r.at[px], along_x(px)).wait_send()
        remote(ad.at[px], ad.at[px], xa_s.at[px], xa_r.at[px], along_x(px)).wait_send()
        remote(r1.at[pf], r1.at[pf], s1_s.at[pf], s1_r.at[pf], along_first(pf)).wait_send()
        remote(r2.at[ps], r2.at[ps], s2_s.at[ps], s2_r.at[ps], along_second(ps)).wait_send()
        remote(spot, spot, s3_s.at[ps], s3_r.at[ps], along_second(ps)).wait_send()
        remote(whole, whole, s4_s.at[pf], s4_r.at[pf], along_first(pf)).wait_send()
        for pc in range(2):
            slot = 2 * py + pc
            remote(
                rd.at[slot], rd.at[slot], dw_s.at[slot], dw_r.at[slot], at(x, py, pc, z)
            ).wait_send()

    loop(1, n, drain_plane)

    def drain_line(d):
        p = lax.rem(z + d, nz)
        remote(ry.at[p], ry.at[p], z_s.at[p], z_r.at[p], at(x, y, c, p)).wait_send()

    loop(1, nz, drain_line)
    for m in range(blocks):
        pz = c * blocks + m
        remote(
            ys.at[m, 1], ryh.at[z], yh_s.at[2 * m + 1], yh_r.at[z], at(x, y, o, pz)
        ).wait_send()

        @pl.when(pz != z)
        def _():
            remote(
                ys.at[m, 0], ryh.at[z], yh_s.at[2 * m], yh_r.at[z], at(x, y, c, pz)
            ).wait_send()


def solution(mesh):
    nz = mesh.shape["hidden"]
    n = 1
    while 2 * n * n < mesh.shape["expert"]:
        n += 1

    def body(weight, scales, act_own, dy_own, own_count, act_help, dy_help, help_count, hot):
        ff, depth = weight.shape[1:]
        rows, hrows = act_own.shape[1], act_help.shape[1]
        half, zblock, xblock = depth // 2, depth // nz, depth // n
        cols, chunk = xblock // (2 * n), 2 * ff // n
        tiles = half // LANES
        groups = min(4, n)
        blocks = half // zblock
        vmem = pltpu.VMEM
        dma = pltpu.SemaphoreType.DMA
        smem = pl.BlockSpec(memory_space=pltpu.SMEM)
        near = pl.BlockSpec(memory_space=pltpu.VMEM)
        far = pl.BlockSpec(memory_space=pl.ANY)
        outs = pl.pallas_call(
            functools.partial(kernel, (n, nz, ff, rows, hrows, depth)),
            out_shape=(
                jax.ShapeDtypeStruct((rows, zblock), BF16),
                jax.ShapeDtypeStruct((rows, ff), BF16),
                jax.ShapeDtypeStruct((ff, depth), BF16),
                jax.ShapeDtypeStruct((hrows, zblock), BF16),
                jax.ShapeDtypeStruct((hrows, ff), BF16),
                jax.ShapeDtypeStruct((ff, cols), F32),
            ),
            in_specs=[smem] * 4 + [near] * 2 + [far] * 3,
            out_specs=(near, near, far, near, near, near),
            scratch_shapes=[
                vmem((ff, depth), BF16),
                vmem((rows, depth), BF16),
                vmem((ff, depth), BF16),
                vmem((rows, ff), BF16),
                vmem((2 * hrows, ff), BF16),
                vmem((2 * hrows, half), BF16),
                vmem((tiles, ff, LANES), BF16),
                vmem((tiles, ff, LANES), BF16),
                vmem((tiles, ff, LANES), BF16),
                vmem((n, 2, ff, LANES), BF16),
                vmem((2, ff, LANES), BF16),
                vmem((n, chunk, LANES), BF16),
                vmem((tiles, ff, LANES), BF16),
                vmem((nz, rows, zblock), BF16),
                vmem((nz, rows, zblock), BF16),
                vmem((ff, depth), BF16),
                vmem((n, hrows, xblock), BF16),
                vmem((n, hrows, ff), BF16),
                vmem((xblock, ff), F32),
                vmem((2 * n, cols, ff), F32),
                vmem((blocks, 2, hrows, zblock), BF16),
                vmem((nz, hrows, zblock), BF16),
                vmem((hrows, ff), F32),
                vmem((hrows, ff), F32),
                dma((6,)),
                dma((groups,)), dma((groups,)),
                dma((2,)), dma((2,)),
                dma((n,)), dma((n,)),
                dma((n,)), dma((n,)),
                dma((nz,)), dma((nz,)),
                dma((n,)), dma((n,)),
                dma((n,)), dma((n,)),
                dma((n,)), dma((n,)),
                dma((n,)), dma((n,)),
                dma((2 * n,)), dma((2 * n,)),
                dma((2 * blocks,)), dma((nz,)),
                dma((1,)), dma((1,)),
            ],
            compiler_params=pltpu.CompilerParams(collective_id=0, has_side_effects=True),
            name="moe_step",
        )(
            hot, own_count, help_count, scales[0], act_own[0], act_help[0],
            weight[0], dy_own[0], dy_help[0],
        )
        own, dact_own, own_grad, helped, dact_help, hot_grad = outs
        return own[None], dact_own[None], own_grad[None], helped[None], dact_help[None], hot_grad

    return jax.shard_map(
        body,
        mesh=mesh,
        in_specs=(
            P("expert", "hidden", None),
            P("expert", None, None),
            P("expert", None, "hidden"),
            P("expert", None, None),
            P("expert"),
            P("expert", None, "hidden"),
            P("expert", None, None),
            P("expert"),
            P(),
        ),
        out_specs=(
            P("expert", None, "hidden"),
            P("expert", None, "hidden"),
            P("expert", "hidden", None),
            P("expert", None, "hidden"),
            P("expert", None, "hidden"),
            P("hidden", "expert"),
        ),
        check_vma=False,
    )
```

```python
import functools

import jax
import jax.numpy as jnp
from jax import lax
from jax.experimental import pallas as pl
from jax.experimental.pallas import tpu as pltpu
from jax.sharding import PartitionSpec as P

MESH = pl.DeviceIdType.MESH
BF16 = jnp.bfloat16
F32 = jnp.float32
LANES = 128
NT = (((1,), (1,)), ((), ()))
TN = (((0,), (0,)), ((), ()))


def kernel(
    cfg,
    hot_h, own_count_h, help_count_h, scales_h, act_own_h, act_help_h, weight, dy_own, dy_help,
    y_own, dact_own, y_help, dact_help, hot_grad,
    hot, own_count, help_count, scales, ao_v, ah_v,
    w_v, dyo_v, deq, own_a, pairs_a, pairs_g, mine, give, got, r1, s2, r2, wf,
    yp, ry, gd, ad, dw, rd, ys, ryh, da_give, da_got,
    load_sem, ex_s, ex_r, pair_s, pair_r, xa_s, xa_r, xg_s, xg_r, fa_s, fa_r, z_s, z_r,
    s1_s, s1_r, s2_s, s2_r, s3_s, s3_r, s4_s, s4_r, dw_s, dw_r, yh_s, yh_r, da_s, da_r,
):
    n, nz, ff, rows, hrows, depth = cfg
    half = depth // 2
    zblock = depth // nz
    xblock = depth // n
    xhalf = xblock // 2
    cols = xblock // (2 * n)
    chunk = 2 * ff // n
    per = ff // chunk
    both = 2 if per > 1 else 1
    parts = n // both
    tall = both * chunk
    e, z = lax.axis_index("expert"), lax.axis_index("hidden")
    x, y, c = lax.div(e, 2 * n), lax.rem(lax.div(e, 2), n), lax.rem(e, 2)
    o = 1 - c

    def at(px, py, pc, pz):
        return ((px * n + py) * 2 + pc, pz)

    first = o * x + c * y
    second = o * y + c * x
    first_p = o * y + c * x

    def along_first(p):
        return at(o * p + c * x, o * y + c * p, c, z)

    def along_second(p):
        return at(o * x + c * p, o * p + c * y, c, z)

    def along_x(p):
        return at(p, y, c, z)

    partner = at(x, y, o, z)

    def loop(low, high, body):
        def step(i, carry):
            body(i)
            return carry

        lax.fori_loop(low, high, step, 0)

    def nth(i, count):
        turn = jnp.where(lax.rem(i, 2) == 0, lax.div(i, 2) + 1, count - lax.div(i + 1, 2))
        return jnp.where(i == count - 1, 0, turn)

    def remote(src, dst, send, recv, device):
        return pltpu.make_async_remote_copy(
            src_ref=src, dst_ref=dst, send_sem=send, recv_sem=recv,
            device_id=device, device_id_type=MESH,
        )

    col_p = pl.multiple_of(o * half, half)
    col_m = pl.multiple_of(c * half, half)
    col_x = pl.multiple_of(x * xblock + c * xhalf, xhalf)

    def local(src, dst, sem):
        return pltpu.make_async_copy(src, dst, load_sem.at[sem])

    load_ah = local(act_help_h, ah_v, 0)
    load_hc = local(help_count_h, help_count, 1)
    load_hot = local(hot_h, hot, 2)
    load_sc = local(scales_h, scales, 3)
    load_wp = local(weight.at[:, pl.ds(col_p, half)], w_v.at[:, pl.ds(col_p, half)], 4)
    load_wm = local(weight.at[:, pl.ds(col_m, half)], w_v.at[:, pl.ds(col_m, half)], 5)
    load_ao = local(act_own_h, ao_v, 6)
    load_oc = local(own_count_h, own_count, 7)
    load_g = local(dy_help.at[:, pl.ds(col_m, half)], pairs_g.at[pl.ds(0, hrows)], 8)
    load_gd = local(dy_help.at[:, pl.ds(col_x, xhalf)], gd.at[c, x], 9)
    load_dyo = local(dy_own, dyo_v, 10)
    for load in (load_ah, load_hc, load_hot, load_sc, load_wp, load_wm):
        load.start()
    for load in (load_ao, load_oc, load_gd, load_g, load_dyo):
        load.start()

    barrier = pltpu.get_barrier_semaphore()

    def greet(device):
        pl.semaphore_signal(barrier, inc=1, device_id=device, device_id_type=MESH)

    def greet_plane(d):
        px, py = lax.rem(x + d, n), lax.rem(y + d, n)
        for pc in range(2):
            greet(at(px, y, pc, z))
            greet(at(x, py, pc, z))

    def greet_line(d):
        pz = lax.rem(z + d, nz)
        for pc in range(2):
            greet(at(x, y, pc, pz))

    greet(partner)
    loop(1, n, greet_plane)
    loop(1, nz, greet_line)

    load_ah.wait()
    load_hc.wait()
    live_help = lax.broadcasted_iota(jnp.int32, (hrows, ff), 0) < help_count[0]
    help_a = jnp.where(live_help, ah_v[...].astype(F32), 0.0).astype(BF16)
    pairs_a[pl.ds(0, hrows), :] = help_a
    ad[c, x] = help_a

    load_hot.wait()
    load_sc.wait()
    flag = jnp.where(hot[0] == e, 1.0, 0.0).astype(F32)

    def scaled(col_base, at_first, dest, i):
        t = lax.rem(at_first + nth(i, n), n)
        for k in range(2):
            tile = lax.div(col_base, LANES) + 2 * t + k
            col = pl.multiple_of(tile * LANES, LANES)
            for part in range(3):
                third = ff // 3
                span = pl.ds(part * third, third)
                scale = scales[lax.div(3 * z + part, 2), 0, tile]
                wide = w_v[span, pl.ds(col, LANES)].astype(F32) * scale
                deq[span, pl.ds(col, LANES)] = wide.astype(BF16)
                dest[2 * i + k, span, :] = (wide * flag).astype(BF16)

    groups = min(4, n)
    each = n // groups

    pl.semaphore_wait(barrier, 4 * (n - 1) + 2 * (nz - 1) + 1)

    def send_a(i):
        p = lax.rem(x + nth(i, n), n)
        remote(
            pairs_a.at[pl.ds(0, hrows)], ad.at[c, x], xa_s.at[p], xa_r.at[x], along_x(p)
        ).start()

    pair_g = remote(
        dy_help.at[:, pl.ds(col_p, half)], pairs_g.at[pl.ds(hrows, hrows)],
        pair_s.at[0], pair_r.at[0], partner,
    )
    pair_a = remote(
        pairs_a.at[pl.ds(0, hrows)], pairs_a.at[pl.ds(hrows, hrows)],
        pair_s.at[1], pair_r.at[1], partner,
    )
    loop(0, n - 1, send_a)

    load_wp.wait()

    def exchange(q):
        tiles = pl.ds(q * 2 * each, 2 * each)
        return remote(give.at[tiles], got.at[tiles], ex_s.at[q], ex_r.at[q], partner)

    def give_group(q):
        for j in range(each):
            scaled(col_p, first_p, give, q * each + j)
        exchange(q).start()

    loop(0, groups, give_group)
    load_wm.wait()
    loop(0, n, functools.partial(scaled, col_m, first, mine))

    for q in range(groups):
        exchange(q).wait_recv()

    def merge(i):
        tiles = pl.ds(2 * i, 2)
        mine[tiles] = mine[tiles] + got[tiles]

    loop(0, n - 1, merge)
    r1[first] = mine[pl.ds(2 * n - 2, 2)] + got[pl.ds(2 * n - 2, 2)]
    high = ff // tall

    def strip(h):
        return lax.div(h, high), pl.ds(pl.multiple_of(lax.rem(h, high) * tall, 16), tall)

    def send_first(j):
        h, i = lax.div(j, n - 1), lax.rem(j, n - 1)
        t = lax.rem(first + nth(i, n), n)
        k, span = strip(h)
        remote(
            mine.at[2 * i + k, span], r1.at[first, k, span], s1_s.at[t], s1_r.at[first, h],
            along_first(t),
        ).start()

    loop(0, parts * (n - 1), send_first)

    def send_g(i):
        p = lax.rem(x + nth(i, n), n)
        for pc in range(2):
            block = pl.ds(pl.multiple_of(p * xblock + pc * xhalf, xhalf), xhalf)
            remote(
                dy_help.at[:, block], gd.at[c, x], xg_s.at[2 * p + pc], xg_r.at[2 * x + c],
                at(p, y, pc, z),
            ).start()

    loop(0, n - 1, send_g)
    block_o = pl.ds(pl.multiple_of(x * xblock + o * xhalf, xhalf), xhalf)
    gd_pair = remote(
        dy_help.at[:, block_o], gd.at[c, x], xg_s.at[2 * x + o], xg_r.at[2 * x + c], partner
    )
    gd_pair.start()
    pair_g.start()
    pair_a.start()

    load_ao.wait()
    load_oc.wait()
    live_own = lax.broadcasted_iota(jnp.int32, (ff, rows), 1) < own_count[0]
    own_a[...] = jnp.where(live_own, ao_v[...].astype(F32), 0.0).T.astype(BF16)

    def own_partial(pz):
        block = pl.ds(pl.multiple_of(pz * zblock, zblock), zblock)
        return jnp.dot(own_a[...], deq[:, block], preferred_element_type=F32).astype(BF16)

    def send_z(i):
        pz = lax.rem(z + nth(i, nz), nz)
        yp[pz] = own_partial(pz)
        remote(yp.at[pz], ry.at[z], z_s.at[pz], z_r.at[z], at(x, y, c, pz)).start()

    loop(0, nz - 1, send_z)
    ry[z] = own_partial(z)

    def wait_a(d):
        p = lax.rem(x + d, n)
        remote(ad.at[c, p], ad.at[c, p], xa_s.at[p], xa_r.at[p], along_x(p)).wait_recv()

    loop(1, n, wait_a)
    forward_a = remote(ad.at[c], ad.at[c], fa_s.at[0], fa_r.at[0], partner)
    forward_a.start()

    load_dyo.wait()
    kblock = 512

    def dact_step(j, total):
        block = pl.ds(pl.multiple_of(j * kblock, kblock), kblock)
        return total + lax.dot_general(
            deq[:, block], dyo_v[:, block], NT, preferred_element_type=F32
        )

    total = lax.fori_loop(0, depth // kblock, dact_step, jnp.zeros((ff, rows), F32))
    dact_own[...] = jnp.where(live_own, total, 0.0).astype(BF16)

    def place(s):
        return lax.div(s, per), pl.ds(pl.multiple_of(lax.rem(s, per) * chunk, 16), chunk)

    def spot(s):
        k, span = place(s)
        return wf.at[2 * first + k, span]

    def send_last(s):
        there = spot(s)

        def send(i):
            p = lax.rem(first + nth(i, n), n)
            remote(there, there, s4_s.at[p], s4_r.at[first], along_first(p)).start()

        loop(0, n - 1, send)

    def reduce_part(h):
        k, span = strip(h)

        def wait_first(d):
            p = lax.rem(first + d, n)
            there = r1.at[p, k, span]
            remote(there, there, s1_s.at[p], s1_r.at[p, h], along_first(p)).wait_recv()

        loop(1, n, wait_first)
        piece = r1[0, k, span, :].astype(F32)
        for p in range(1, n):
            piece = piece + r1[p, k, span, :].astype(F32)
        s2[k, span, :] = piece.astype(BF16)
        for j in range(both):
            s = both * h + j
            pk, pspan = place(s)

            @pl.when(s != second)
            def _():
                remote(
                    s2.at[pk, pspan], r2.at[second], s2_s.at[s], s2_r.at[second],
                    along_second(s),
                ).start()

            @pl.when(s == second)
            def _():
                r2[second] = piece[j * chunk : (j + 1) * chunk].astype(BF16)

    def reduce_mine():
        def wait_second(d):
            p = lax.rem(second + d, n)
            remote(r2.at[p], r2.at[p], s2_s.at[p], s2_r.at[p], along_second(p)).wait_recv()

        loop(1, n, wait_second)
        piece = r2[0].astype(F32)
        for p in range(1, n):
            piece = piece + r2[p].astype(F32)
        there = spot(second)
        there[...] = piece.astype(BF16)

        def send_third(i):
            p = lax.rem(second + nth(i, n), n)
            remote(there, there, s3_s.at[p], s3_r.at[second], along_second(p)).start()

        loop(0, n - 1, send_third)
        send_last(second)

    def pass_on(s):
        @pl.when(s != second)
        def _():
            there = spot(s)
            remote(there, there, s3_s.at[s], s3_r.at[s], along_second(s)).wait_recv()
            send_last(s)

    def stage(i):
        pl.when(i < parts)(lambda: reduce_part(i))
        pl.when(lax.div(second, both) == i - 2)(reduce_mine)

        @pl.when(i >= 4)
        def _():
            for j in range(both):
                pass_on(both * (i - 4) + j)

    loop(0, parts + 2, stage)

    load_gd.wait()
    forward_a.wait_recv()

    def wait_g(d):
        p = lax.rem(x + d, n)
        for pc in range(2):
            there = gd.at[pc, p]
            remote(there, there, xg_s.at[0], xg_r.at[2 * p + pc], at(p, y, pc, z)).wait_recv()

    loop(1, n, wait_g)
    there = gd.at[o, x]
    remote(there, there, xg_s.at[0], xg_r.at[2 * x + o], partner).wait_recv()
    dw[...] = lax.dot_general(
        gd[...].reshape(2 * n * hrows, xhalf), ad[...].reshape(2 * n * hrows, ff), TN,
        preferred_element_type=F32,
    )
    shared = n // 2

    def each_owner(body):
        def one(i):
            p = c * shared + lax.rem(y + lax.div(i, 2), shared)
            pc = lax.rem(i, 2)
            slot = 2 * lax.rem(y + lax.div(i, 2), shared) + pc
            part = dw.at[pl.ds(pl.multiple_of(slot * cols, cols), cols)]
            copy = remote(part, rd.at[y], dw_s.at[slot], dw_r.at[y], at(x, p, pc, z))
            body(copy, part, (p == y) & (pc == c))

        loop(0, n, one)

    def send_dw(copy, part, own):
        pl.when(jnp.logical_not(own))(copy.start)

        @pl.when(own)
        def _():
            rd[y] = part[...]

    each_owner(send_dw)

    loop(parts + 2, parts + 4, stage)

    def wait_z(d):
        p = lax.rem(z + d, nz)
        remote(ry.at[p], ry.at[p], z_s.at[p], z_r.at[p], at(x, y, c, p)).wait_recv()

    loop(1, nz, wait_z)

    def sum_z(i):
        span = pl.ds(pl.multiple_of(i * 16, 16), 16)
        piece = ry[0, span, :].astype(F32)
        for p in range(1, nz):
            piece = piece + ry[p, span, :].astype(F32)
        y_own[span, :] = piece.astype(BF16)

    loop(0, rows // 16, sum_z)

    load_g.wait()
    pair_g.wait_recv()
    pair_a.wait_recv()
    blocks = half // zblock
    tiles_per = zblock // LANES

    def wait_fourth(p):
        there = wf.at[pl.ds(2 * p, 2)]
        remote(there, there, s4_s.at[p], s4_r.at[p], along_first(p)).wait_recv()

    da = jnp.zeros((2 * hrows, ff), F32)
    for m in range(blocks):
        pz = c * blocks + m
        for p in range(m * tiles_per // 2, (m + 1) * tiles_per // 2):
            pl.when(first != p)(functools.partial(wait_fourth, p))
        block = jnp.concatenate([wf[m * tiles_per + j] for j in range(tiles_per)], axis=1)
        out = jnp.dot(pairs_a[...], block, preferred_element_type=F32).astype(BF16)
        ys[m] = out.reshape(2, hrows, zblock)
        remote(
            ys.at[m, 1], ryh.at[z], yh_s.at[2 * m + 1], yh_r.at[z], at(x, y, o, pz)
        ).start()

        @pl.when(pz != z)
        def _():
            remote(
                ys.at[m, 0], ryh.at[z], yh_s.at[2 * m], yh_r.at[z], at(x, y, c, pz)
            ).start()

        @pl.when(pz == z)
        def _():
            ryh[z] = ys[m, 0]

        da = da + lax.dot_general(
            pairs_g[:, m * zblock : (m + 1) * zblock], block, NT, preferred_element_type=F32
        )
    da_give[...] = da[hrows:]
    da_copy = remote(da_give, da_got, da_s.at[0], da_r.at[0], partner)
    da_copy.start()

    owner = lax.div(y, shared)

    def wait_dw(p):
        @pl.when((p != y) | (owner != c))
        def _():
            there = rd.at[p]
            remote(there, there, dw_s.at[0], dw_r.at[p], at(x, p, owner, z)).wait_recv()

    loop(0, n, wait_dw)
    total = rd[0]
    for p in range(1, n):
        total = total + rd[p]
    hot_grad[...] = total

    source = lax.div(z, blocks)

    def wait_yh(p):
        @pl.when((p != z) | (source != c))
        def _():
            remote(
                ryh.at[p], ryh.at[p], yh_s.at[0], yh_r.at[p], at(x, y, source, p)
            ).wait_recv()

    da_copy.wait_recv()
    dact_help[...] = jnp.where(live_help, da[:hrows] + da_got[...], 0.0).astype(BF16)

    loop(0, nz, wait_yh)
    piece = ryh[0].astype(F32)
    for p in range(1, nz):
        piece = piece + ryh[p].astype(F32)
    y_help[...] = piece.astype(BF16)

    for copy in (pair_a, pair_g, gd_pair, forward_a, da_copy):
        copy.wait_send()

    def drain_exchange(q):
        exchange(q).wait_send()

    loop(0, groups, drain_exchange)
    mine_spot = spot(second)

    def drain_plane(d):
        px, pf, ps = (lax.rem(v + d, n) for v in (x, first, second))
        for pc in range(2):
            there = gd.at[c, px]
            remote(there, there, xg_s.at[2 * px + pc], xg_r.at[0], at(px, y, pc, z)).wait_send()
        there = ad.at[c, px]
        remote(there, there, xa_s.at[px], xa_r.at[px], along_x(px)).wait_send()
        remote(r1.at[pf], r1.at[pf], s1_s.at[pf], s1_r.at[pf, 0], along_first(pf)).wait_send()
        remote(r2.at[ps], r2.at[ps], s2_s.at[ps], s2_r.at[ps], along_second(ps)).wait_send()
        remote(mine_spot, mine_spot, s3_s.at[ps], s3_r.at[ps], along_second(ps)).wait_send()
        there = wf.at[pl.ds(2 * first, 2)]
        remote(there, there, s4_s.at[pf], s4_r.at[pf], along_first(pf)).wait_send()

    loop(1, n, drain_plane)
    each_owner(lambda copy, part, own: pl.when(jnp.logical_not(own))(copy.wait_send))

    def drain_line(d):
        p = lax.rem(z + d, nz)
        remote(ry.at[p], ry.at[p], z_s.at[p], z_r.at[p], at(x, y, c, p)).wait_send()

    loop(1, nz, drain_line)
    for m in range(blocks):
        pz = c * blocks + m
        remote(
            ys.at[m, 1], ryh.at[z], yh_s.at[2 * m + 1], yh_r.at[z], at(x, y, o, pz)
        ).wait_send()

        @pl.when(pz != z)
        def _():
            remote(
                ys.at[m, 0], ryh.at[z], yh_s.at[2 * m], yh_r.at[z], at(x, y, c, pz)
            ).wait_send()


def finish(
    own_count, act, dy, y_in, da_in, yh_in, dah_in, hg_in, grad, y_out, da_out, yh_out, dah_out,
    hg_out,
):
    live = lax.broadcasted_iota(jnp.int32, act.shape, 1) < own_count[0]
    rows = jnp.where(live, act[...].astype(F32), 0.0).astype(BF16)
    grad[...] = jnp.dot(rows, dy[...], preferred_element_type=F32).astype(BF16)

    @pl.when(pl.program_id(0) == 0)
    def _():
        y_out[...] = y_in[...]
        da_out[...] = da_in[...]
        yh_out[...] = yh_in[...]
        dah_out[...] = dah_in[...]
        hg_out[...] = hg_in[...]


def solution(mesh):
    nz = mesh.shape["hidden"]
    n = 1
    while 2 * n * n < mesh.shape["expert"]:
        n += 1

    def body(weight, scales, act_own, dy_own, own_count, act_help, dy_help, help_count, hot):
        ff, depth = weight.shape[1:]
        rows, hrows = act_own.shape[1], act_help.shape[1]
        half, zblock, xblock = depth // 2, depth // nz, depth // n
        cols, chunk = xblock // (2 * n), 2 * ff // n
        tiles = half // LANES
        groups = min(4, n)
        blocks = half // zblock
        vmem = pltpu.VMEM
        dma = pltpu.SemaphoreType.DMA
        smem = pl.BlockSpec(memory_space=pltpu.SMEM)
        near = pl.BlockSpec(memory_space=pltpu.VMEM)
        far = pl.BlockSpec(memory_space=pl.ANY)
        act_t = jnp.swapaxes(act_own, 1, 2)[0]
        mid = (
            jax.ShapeDtypeStruct((rows, zblock), BF16),
            jax.ShapeDtypeStruct((ff, rows), BF16),
            jax.ShapeDtypeStruct((hrows, zblock), BF16),
            jax.ShapeDtypeStruct((hrows, ff), BF16),
            jax.ShapeDtypeStruct((cols, ff), F32),
        )
        outs = pl.pallas_call(
            functools.partial(kernel, (n, nz, ff, rows, hrows, depth)),
            out_shape=mid,
            in_specs=[pl.BlockSpec(memory_space=pltpu.HBM)] * 4 + [far] * 5,
            out_specs=(near,) * 5,
            scratch_shapes=[
                pltpu.SMEM((1,), jnp.int32),
                pltpu.SMEM((1,), jnp.int32),
                pltpu.SMEM((1,), jnp.int32),
                pltpu.SMEM((scales.shape[1], 1, scales.shape[2]), F32),
                vmem((ff, rows), BF16),
                vmem((hrows, ff), BF16),
                vmem((ff, depth), BF16),
                vmem((rows, depth), BF16),
                vmem((ff, depth), BF16),
                vmem((rows, ff), BF16),
                vmem((2 * hrows, ff), BF16),
                vmem((2 * hrows, half), BF16),
                vmem((tiles, ff, LANES), BF16),
                vmem((tiles, ff, LANES), BF16),
                vmem((tiles, ff, LANES), BF16),
                vmem((n, 2, ff, LANES), BF16),
                vmem((2, ff, LANES), BF16),
                vmem((n, chunk, LANES), BF16),
                vmem((tiles, ff, LANES), BF16),
                vmem((nz, rows, zblock), BF16),
                vmem((nz, rows, zblock), BF16),
                vmem((2, n, hrows, xblock // 2), BF16),
                vmem((2, n, hrows, ff), BF16),
                vmem((xblock // 2, ff), F32),
                vmem((n, cols, ff), F32),
                vmem((blocks, 2, hrows, zblock), BF16),
                vmem((nz, hrows, zblock), BF16),
                vmem((hrows, ff), F32),
                vmem((hrows, ff), F32),
                dma((11,)),
                dma((groups,)), dma((groups,)),
                dma((2,)), dma((2,)),
                dma((n,)), dma((n,)),
                dma((2 * n,)), dma((2 * n,)),
                dma((1,)), dma((1,)),
                dma((nz,)), dma((nz,)),
                dma((n,)), dma((n, n)),
                dma((n,)), dma((n,)),
                dma((n,)), dma((n,)),
                dma((n,)), dma((n,)),
                dma((n,)), dma((n,)),
                dma((2 * blocks,)), dma((nz,)),
                dma((1,)), dma((1,)),
            ],
            compiler_params=pltpu.CompilerParams(collective_id=0, has_side_effects=True),
            name="moe_step",
        )(
            hot, own_count, help_count, jnp.swapaxes(scales, 0, 1), act_t, act_help[0],
            weight[0], dy_own[0], dy_help[0],
        )
        steps = 4
        whole = lambda a: pl.BlockSpec(a.shape, lambda i: (0,) * len(a.shape))
        done = pl.pallas_call(
            finish,
            grid=(steps,),
            out_shape=(jax.ShapeDtypeStruct((ff, depth), BF16), *mid),
            in_specs=[
                smem, whole(act_t), pl.BlockSpec((rows, depth // steps), lambda i: (0, i)),
                *(whole(a) for a in mid),
            ],
            out_specs=(
                pl.BlockSpec((ff, depth // steps), lambda i: (0, i)), *(whole(a) for a in mid)
            ),
            name="finish",
        )(own_count, act_t, dy_own[0], *outs)
        own_grad, own, dact_own, helped, dact_help, hot_grad = done
        dact_own = jnp.swapaxes(dact_own[None], 1, 2)
        return own[None], dact_own, own_grad[None], helped[None], dact_help[None], hot_grad.T

    return jax.shard_map(
        body,
        mesh=mesh,
        in_specs=(
            P("expert", "hidden", None),
            P("expert", None, None),
            P("expert", None, "hidden"),
            P("expert", None, None),
            P("expert"),
            P("expert", None, "hidden"),
            P("expert", None, None),
            P("expert"),
            P(),
        ),
        out_specs=(
            P("expert", None, "hidden"),
            P("expert", None, "hidden"),
            P("expert", "hidden", None),
            P("expert", None, "hidden"),
            P("expert", None, "hidden"),
            P("hidden", "expert"),
        ),
        check_vma=False,
    )
```

```python
import functools

import jax
import jax.numpy as jnp
from jax import lax
from jax.experimental import pallas as pl
from jax.experimental.pallas import tpu as pltpu
from jax.sharding import PartitionSpec as P

MESH = pl.DeviceIdType.MESH
BF16 = jnp.bfloat16
F32 = jnp.float32
LANES = 128
NT = (((1,), (1,)), ((), ()))
TN = (((0,), (0,)), ((), ()))


def kernel(
    cfg,
    hot_h, own_count_h, help_count_h, scales_h, act_own_h, act_help_h, weight, dy_own, dy_help,
    y_own, dact_own, y_help, dact_help, hot_grad,
    hot, own_count, help_count, scales, ao_v, ah_v,
    w_v, dyo_v, deq, own_a, a8, g8, mine, give, got, r1, s2, r2, wb,
    yp, ry, dw, rd, ys, ryh, da_give, da_got,
    load_sem, ex_s, ex_r, xa_s, xa_r, xg_s, xg_r, z_s, z_r,
    s1_s, s1_r, s2_s, s2_r, s4_s, s4_r, dw_s, dw_r, yh_s, yh_r, da_s, da_r,
):
    n, nz, ff, rows, hrows, depth = cfg
    half = depth // 2
    zblock = depth // nz
    wide = depth // 8
    spread = 8 // nz
    owners = 2 * n * n // 8
    cols = wide // owners
    parts = 4
    tall = ff // 2
    e, z = lax.axis_index("expert"), lax.axis_index("hidden")
    x, y, c = lax.div(e, 2 * n), lax.rem(lax.div(e, 2), n), lax.rem(e, 2)
    o = 1 - c

    def at(px, py, pc, pz):
        return ((px * n + py) * 2 + pc, pz)

    first = o * x + c * y
    second = o * y + c * x
    first_p = o * y + c * x

    def along_first(p):
        return at(o * p + c * x, o * y + c * p, c, z)

    def along_second(p):
        return at(o * x + c * p, o * p + c * y, c, z)

    def mate(j, pz):
        return at(
            x - lax.rem(x, 2) + lax.rem(lax.div(j, 2), 2), y - lax.rem(y, 2) + lax.rem(j, 2),
            lax.div(j, 4), pz,
        )

    def block_of(j):
        jc, jx, jy = lax.div(j, 4), lax.rem(lax.div(j, 2), 2), lax.rem(j, 2)
        return 4 * jc + (1 - jc) * (2 * jx + jy) + jc * (2 * jy + jx)

    me = 4 * c + 2 * lax.rem(x, 2) + lax.rem(y, 2)
    mb = block_of(me)

    def holder(b, i):
        f = 2 * lax.div(i, n // 2) + lax.rem(lax.div(b, 2), 2)
        s = 2 * lax.rem(i, n // 2) + lax.rem(b, 2)
        bc = lax.div(b, 4)
        return at((1 - bc) * f + bc * s, (1 - bc) * s + bc * f, bc, z)

    seat = lax.div(first, 2) * (n // 2) + lax.div(second, 2)

    partner = at(x, y, o, z)

    def loop(low, high, body):
        def step(i, carry):
            body(i)
            return carry

        lax.fori_loop(low, high, step, 0)

    def nth(i, count):
        turn = jnp.where(lax.rem(i, 2) == 0, lax.div(i, 2) + 1, count - lax.div(i + 1, 2))
        return jnp.where(i == count - 1, 0, turn)

    def remote(src, dst, send, recv, device):
        return pltpu.make_async_remote_copy(
            src_ref=src, dst_ref=dst, send_sem=send, recv_sem=recv,
            device_id=device, device_id_type=MESH,
        )

    col_p = pl.multiple_of(o * half, half)
    col_m = pl.multiple_of(c * half, half)
    col_b = pl.multiple_of(mb * wide, wide)

    def local(src, dst, sem):
        return pltpu.make_async_copy(src, dst, load_sem.at[sem])

    load_ah = local(act_help_h, ah_v, 0)
    load_hc = local(help_count_h, help_count, 1)
    load_hot = local(hot_h, hot, 2)
    load_sc = local(scales_h, scales, 3)
    load_wp = local(weight.at[:, pl.ds(col_p, half)], w_v.at[:, pl.ds(col_p, half)], 4)
    load_wm = local(weight.at[:, pl.ds(col_m, half)], w_v.at[:, pl.ds(col_m, half)], 5)
    load_ao = local(act_own_h, ao_v, 6)
    load_oc = local(own_count_h, own_count, 7)
    load_g = local(dy_help.at[:, pl.ds(col_b, wide)], g8.at[me], 8)
    load_dyo = local(dy_own, dyo_v, 9)
    for load in (load_ah, load_hc, load_hot, load_sc, load_wp, load_wm):
        load.start()
    for load in (load_g, load_ao, load_oc, load_dyo):
        load.start()

    barrier = pltpu.get_barrier_semaphore()

    def greet(device):
        pl.semaphore_signal(barrier, inc=1, device_id=device, device_id_type=MESH)

    def greet_lines(d):
        greet(along_first(lax.rem(first + d, n)))
        greet(along_second(lax.rem(second + d, n)))

    def greet_z(d):
        greet(at(x, y, c, lax.rem(z + d, nz)))

    def greet_mate(d):
        greet(mate(lax.rem(me + d, 8), z))

    my_b = lax.div(e, owners)
    in_b = (mb == my_b).astype(jnp.int32)

    def sender(i):
        b = z * spread + lax.rem(i, spread)
        bc = lax.div(b, 4)
        b1, b0 = lax.rem(lax.div(b, 2), 2), lax.rem(b, 2)
        return 4 * bc + (1 - bc) * (2 * b1 + b0) + bc * (2 * b0 + b1), lax.div(i, spread)

    loop(1, n, greet_lines)
    loop(1, nz, greet_z)
    loop(1, 8, greet_mate)

    load_ah.wait()
    load_hc.wait()
    live_help = lax.broadcasted_iota(jnp.int32, (hrows, ff), 0) < help_count[0]
    help_a = jnp.where(live_help, ah_v[...].astype(F32), 0.0).astype(BF16)
    a8[me] = help_a

    load_hot.wait()
    load_sc.wait()
    flag = jnp.where(hot[0] == e, 1.0, 0.0).astype(F32)

    def tile_of(base, t):
        b = 2 * lax.rem(t, 2) + lax.rem(lax.div(t, 2), 2)
        return base + b * (wide // LANES) + 2 * lax.div(t, 4)

    def scaled(col_base, at_first, dest, i):
        t = lax.rem(at_first + nth(i, n), n)
        for k in range(2):
            tile = tile_of(lax.div(col_base, LANES), t) + k
            col = pl.multiple_of(tile * LANES, LANES)
            for part in range(3):
                third = ff // 3
                span = pl.ds(part * third, third)
                scale = scales[lax.div(3 * z + part, 2), 0, tile]
                wide = w_v[span, pl.ds(col, LANES)].astype(F32) * scale
                deq[span, pl.ds(col, LANES)] = wide.astype(BF16)
                dest[2 * i + k, span, :] = (wide * flag).astype(BF16)

    groups = min(4, n)
    each = n // groups

    pl.semaphore_wait(barrier, 2 * (n - 1) + (nz - 1) + 7)

    def send_mate(d):
        j = lax.rem(me + d, 8)
        remote(a8.at[me], a8.at[me], xa_s.at[j], xa_r.at[me], mate(j, z)).start()
        block = pl.ds(pl.multiple_of(block_of(j) * wide, wide), wide)
        remote(dy_help.at[:, block], g8.at[me], xg_s.at[j], xg_r.at[me], mate(j, z)).start()

    loop(1, 8, send_mate)

    load_wp.wait()

    def exchange(q):
        tiles = pl.ds(q * 2 * each, 2 * each)
        return remote(give.at[tiles], got.at[tiles], ex_s.at[q], ex_r.at[q], partner)

    def give_group(q):
        for j in range(each):
            scaled(col_p, first_p, give, q * each + j)
        exchange(q).start()

    loop(0, groups, give_group)
    load_wm.wait()
    loop(0, n, functools.partial(scaled, col_m, first, mine))

    for q in range(groups):
        exchange(q).wait_recv()

    def merge(i):
        tiles = pl.ds(2 * i, 2)
        mine[tiles] = mine[tiles] + got[tiles]

    loop(0, n - 1, merge)
    r1[first] = mine[pl.ds(2 * n - 2, 2)] + got[pl.ds(2 * n - 2, 2)]
    high = 2

    def strip(h):
        return lax.div(h, high), pl.ds(pl.multiple_of(lax.rem(h, high) * tall, 16), tall)

    def send_first(j):
        h, i = lax.div(j, n - 1), lax.rem(j, n - 1)
        t = lax.rem(first + nth(i, n), n)
        k, span = strip(h)
        remote(
            mine.at[2 * i + k, span], r1.at[first, k, span], s1_s.at[t], s1_r.at[first, h],
            along_first(t),
        ).start()

    loop(0, parts * (n - 1), send_first)

    load_ao.wait()
    load_oc.wait()
    live_own = lax.broadcasted_iota(jnp.int32, (ff, rows), 1) < own_count[0]
    own_a[...] = jnp.where(live_own, ao_v[...].astype(F32), 0.0).T.astype(BF16)

    def own_partial(pz):
        block = pl.ds(pl.multiple_of(pz * zblock, zblock), zblock)
        return jnp.dot(own_a[...], deq[:, block], preferred_element_type=F32).astype(BF16)

    def send_z(i):
        pz = lax.rem(z + nth(i, nz), nz)
        yp[pz] = own_partial(pz)
        remote(yp.at[pz], ry.at[z], z_s.at[pz], z_r.at[z], at(x, y, c, pz)).start()

    loop(0, nz - 1, send_z)
    ry[z] = own_partial(z)

    load_dyo.wait()
    kblock = 512

    def dact_step(j, total):
        block = pl.ds(pl.multiple_of(j * kblock, kblock), kblock)
        return total + lax.dot_general(
            deq[:, block], dyo_v[:, block], NT, preferred_element_type=F32
        )

    total = lax.fori_loop(0, depth // kblock, dact_step, jnp.zeros((ff, rows), F32))
    dact_own[...] = jnp.where(live_own, total, 0.0).astype(BF16)

    parity = lax.rem(lax.div(first, 2), 2)
    keeps = parity == lax.rem(second, 2)
    u = lax.div(first, 4)

    def reduce_part(h):
        k, span = strip(h)

        def wait_first(d):
            p = lax.rem(first + d, n)
            there = r1.at[p, k, span]
            remote(there, there, s1_s.at[p], s1_r.at[p, h], along_first(p)).wait_recv()

        loop(1, n, wait_first)
        piece = r1[0, k, span, :].astype(F32)
        for p in range(1, n):
            piece = piece + r1[p, k, span, :].astype(F32)
        s2[k, span, :] = piece.astype(BF16)

        def send_second(i):
            p = lax.rem(2 * i + second - lax.rem(second, 2) + parity, n)

            @pl.when(p != second)
            def _():
                remote(
                    s2.at[k, span], r2.at[second, k, span], s2_s.at[p], s2_r.at[second, h],
                    along_second(p),
                ).start()

        loop(0, n // 2, send_second)

        @pl.when(keeps)
        def _():
            r2[second, k, span, :] = piece.astype(BF16)

    def keep_part(h):
        k, span = strip(h)

        def wait_second(d):
            p = lax.rem(second + d, n)
            there = r2.at[p, k, span]
            remote(there, there, s2_s.at[p], s2_r.at[p, h], along_second(p)).wait_recv()

        loop(1, n, wait_second)
        piece = r2[0, k, span, :].astype(F32)
        for p in range(1, n):
            piece = piece + r2[p, k, span, :].astype(F32)
        there = wb.at[u, k, span]
        there[...] = piece.astype(BF16)

        def send_last(i):
            p = lax.rem(first + 2 * i, n)
            remote(there, there, s4_s.at[p], s4_r.at[u], along_first(p)).start()

        loop(1, n // 2, send_last)

    def stage(i):
        pl.when(i < parts)(lambda: reduce_part(i))
        pl.when((i >= 2) & keeps)(lambda: keep_part(i - 2))

    loop(0, parts, stage)

    loop(parts, parts + 2, stage)

    load_g.wait()

    def wait_mate(d):
        j = lax.rem(me + d, 8)
        remote(a8.at[j], a8.at[j], xa_s.at[j], xa_r.at[j], mate(j, z)).wait_recv()
        remote(g8.at[j], g8.at[j], xg_s.at[j], xg_r.at[j], mate(j, z)).wait_recv()

    loop(1, 8, wait_mate)
    dw[...] = lax.dot_general(
        g8[...].reshape(8 * hrows, wide), a8[...].reshape(8 * hrows, ff), TN,
        preferred_element_type=F32,
    ).astype(BF16)

    def each_owner(body):
        def one(d):
            i = lax.rem(seat + d, owners)
            part = dw.at[pl.ds(pl.multiple_of(i * cols, cols), cols)]
            owner = mb * owners + i
            copy = remote(part, rd.at[seat], dw_s.at[i], dw_r.at[seat], (owner, z))
            body(copy, part, owner == e)

        loop(0, owners, one)

    def send_dw(copy, part, own):
        pl.when(jnp.logical_not(own))(copy.start)

        @pl.when(own)
        def _():
            rd[seat] = part[...]

    each_owner(send_dw)

    def wait_z(d):
        p = lax.rem(z + d, nz)
        remote(ry.at[p], ry.at[p], z_s.at[p], z_r.at[p], at(x, y, c, p)).wait_recv()

    loop(1, nz, wait_z)

    def sum_z(i):
        span = pl.ds(pl.multiple_of(i * 16, 16), 16)
        piece = ry[0, span, :].astype(F32)
        for p in range(1, nz):
            piece = piece + ry[p, span, :].astype(F32)
        y_own[span, :] = piece.astype(BF16)

    loop(0, rows // 16, sum_z)

    for i in range(n // 4):
        t = lax.rem(first, 2) + 2 * lax.rem(second, 2) + 4 * i

        @pl.when(t != first)
        def _():
            remote(wb.at[i], wb.at[i], s4_s.at[t], s4_r.at[i], along_first(t)).wait_recv()

    block = jnp.concatenate([wb[j // 2, j % 2] for j in range(n // 2)], axis=1)
    out = jnp.dot(a8[...].reshape(8 * hrows, ff), block, preferred_element_type=F32)
    ys[...] = out.astype(BF16).reshape(8, hrows, wide)
    pz = lax.div(mb, spread)
    sub = lax.rem(mb, spread)
    landing = pl.ds(pl.multiple_of(sub * wide, wide), wide)

    def helped(j):
        return remote(
            ys.at[j], ryh.at[z, :, landing], yh_s.at[j], yh_r.at[z, sub], mate(j, pz)
        )

    def send_helped(d):
        j = lax.rem(me + d, 8)
        own = (j == me) & (pz == z)
        pl.when(jnp.logical_not(own))(helped(j).start)

        @pl.when(own)
        def _():
            ryh[z, :, landing] = ys[j]

    loop(0, 8, send_helped)
    da = lax.dot_general(
        g8[...].reshape(8 * hrows, wide), block, NT, preferred_element_type=F32
    )
    da_give[...] = da.astype(BF16).reshape(8, hrows, ff)

    def da_copy(j):
        return remote(da_give.at[j], da_got.at[me], da_s.at[j], da_r.at[me], mate(j, z))

    loop(1, 8, lambda d: da_copy(lax.rem(me + d, 8)).start())
    da_got[me] = da_give[me]

    def wait_dw(i):
        @pl.when((i != seat) | (in_b == 0))
        def _():
            remote(rd.at[i], rd.at[i], dw_s.at[i], dw_r.at[i], holder(my_b, i)).wait_recv()

    loop(0, owners, wait_dw)
    total = rd[0].astype(F32)
    for p in range(1, owners):
        total = total + rd[p].astype(F32)
    hot_grad[...] = total

    def wait_da(d):
        j = lax.rem(me + d, 8)
        remote(da_got.at[j], da_got.at[j], da_s.at[j], da_r.at[j], mate(j, z)).wait_recv()

    loop(1, 8, wait_da)
    total = da_got[0].astype(F32)
    for j in range(1, 8):
        total = total + da_got[j].astype(F32)
    dact_help[...] = jnp.where(live_help, total, 0.0).astype(BF16)

    def wait_helped(i):
        j, p = sender(i)

        @pl.when((j != me) | (p != z))
        def _():
            s = lax.rem(i, spread)
            there = ryh.at[p, :, pl.ds(pl.multiple_of(s * wide, wide), wide)]
            remote(there, there, yh_s.at[0], yh_r.at[p, s], mate(j, p)).wait_recv()

    loop(0, 8, wait_helped)
    piece = ryh[0].astype(F32)
    for p in range(1, nz):
        piece = piece + ryh[p].astype(F32)
    y_help[...] = piece.astype(BF16)

    def drain_exchange(q):
        exchange(q).wait_send()

    loop(0, groups, drain_exchange)

    def drain_mate(d):
        j = lax.rem(me + d, 8)
        remote(a8.at[j], a8.at[j], xa_s.at[j], xa_r.at[j], mate(j, z)).wait_send()
        remote(g8.at[j], g8.at[j], xg_s.at[j], xg_r.at[j], mate(j, z)).wait_send()
        da_copy(j).wait_send()

    loop(1, 8, drain_mate)

    def drain_first(d):
        p = lax.rem(first + d, n)
        remote(r1.at[p], r1.at[p], s1_s.at[p], s1_r.at[p, 0], along_first(p)).wait_send()

    loop(1, n, drain_first)

    def drain_second(i):
        p = lax.rem(2 * i + second - lax.rem(second, 2) + parity, n)

        @pl.when(p != second)
        def _():
            remote(r2.at[p], r2.at[p], s2_s.at[p], s2_r.at[p, 0], along_second(p)).wait_send()

        @pl.when(keeps & (i > 0))
        def _():
            p = lax.rem(first + 2 * i, n)
            remote(wb.at[u], wb.at[u], s4_s.at[p], s4_r.at[u], along_first(p)).wait_send()

    loop(0, n // 2, drain_second)
    each_owner(lambda copy, part, own: pl.when(jnp.logical_not(own))(copy.wait_send))

    def drain_line(d):
        p = lax.rem(z + d, nz)
        remote(ry.at[p], ry.at[p], z_s.at[p], z_r.at[p], at(x, y, c, p)).wait_send()

    loop(1, nz, drain_line)

    def drain_helped(j):
        pl.when((j != me) | (pz != z))(helped(j).wait_send)

    loop(0, 8, drain_helped)


def finish(*refs):
    own_count, act, dy = refs[:3]
    mids, grad, outs = refs[3:8], refs[8], refs[9:14]
    act_v, dy_v, grad_v, held, sem = refs[14], refs[15], refs[16], refs[17:22], refs[22]
    steps = 4
    width = dy.shape[1] // steps

    def part(ref, j):
        return ref.at[:, pl.ds(j * width, width)]

    def copy(src, dst, i):
        return pltpu.make_async_copy(src, dst, sem.at[i])

    loads = [copy(act, act_v, 0)]
    loads += [copy(part(dy, j), part(dy_v, j), 1 + j) for j in range(steps)]
    takes = [copy(mids[i], held[i], 1 + steps + i) for i in range(5)]
    gives = [copy(held[i], outs[i], 6 + steps + i) for i in range(5)]
    stores = [copy(part(grad_v, j), part(grad, j), 11 + steps + j) for j in range(steps)]
    for load in loads + takes:
        load.start()
    loads[0].wait()
    live = lax.broadcasted_iota(jnp.int32, act.shape, 1) < own_count[0]
    rows = jnp.where(live, act_v[...].astype(F32), 0.0).astype(BF16)
    for j in range(steps):
        loads[1 + j].wait()
        span = pl.ds(j * width, width)
        grad_v[:, span] = jnp.dot(
            rows, dy_v[:, span], preferred_element_type=F32
        ).astype(BF16)
        stores[j].start()
    for take, give in zip(takes, gives):
        take.wait()
        give.start()
    for out in gives + stores:
        out.wait()


def solution(mesh):
    nz = mesh.shape["hidden"]
    n = 1
    while 2 * n * n < mesh.shape["expert"]:
        n += 1

    def body(weight, scales, act_own, dy_own, own_count, act_help, dy_help, help_count, hot):
        ff, depth = weight.shape[1:]
        rows, hrows = act_own.shape[1], act_help.shape[1]
        half, zblock, wide = depth // 2, depth // nz, depth // 8
        owners, cols = n * n // 4, depth // (2 * n * n)
        tiles = half // LANES
        groups = min(4, n)
        vmem = pltpu.VMEM
        dma = pltpu.SemaphoreType.DMA
        smem = pl.BlockSpec(memory_space=pltpu.SMEM)
        near = pl.BlockSpec(memory_space=pltpu.VMEM)
        far = pl.BlockSpec(memory_space=pl.ANY)
        act_t = jnp.swapaxes(act_own, 1, 2)[0]
        mid = (
            jax.ShapeDtypeStruct((rows, zblock), BF16),
            jax.ShapeDtypeStruct((ff, rows), BF16),
            jax.ShapeDtypeStruct((hrows, zblock), BF16),
            jax.ShapeDtypeStruct((hrows, ff), BF16),
            jax.ShapeDtypeStruct((cols, ff), F32),
        )
        outs = pl.pallas_call(
            functools.partial(kernel, (n, nz, ff, rows, hrows, depth)),
            out_shape=mid,
            in_specs=[pl.BlockSpec(memory_space=pltpu.HBM)] * 4 + [far] * 5,
            out_specs=(near,) * 5,
            scratch_shapes=[
                pltpu.SMEM((1,), jnp.int32),
                pltpu.SMEM((1,), jnp.int32),
                pltpu.SMEM((1,), jnp.int32),
                pltpu.SMEM((scales.shape[1], 1, scales.shape[2]), F32),
                vmem((ff, rows), BF16),
                vmem((hrows, ff), BF16),
                vmem((ff, depth), BF16),
                vmem((rows, depth), BF16),
                vmem((ff, depth), BF16),
                vmem((rows, ff), BF16),
                vmem((8, hrows, ff), BF16),
                vmem((8, hrows, wide), BF16),
                vmem((tiles, ff, LANES), BF16),
                vmem((tiles, ff, LANES), BF16),
                vmem((tiles, ff, LANES), BF16),
                vmem((n, 2, ff, LANES), BF16),
                vmem((2, ff, LANES), BF16),
                vmem((n, 2, ff, LANES), BF16),
                vmem((n // 4, 2, ff, LANES), BF16),
                vmem((nz, rows, zblock), BF16),
                vmem((nz, rows, zblock), BF16),
                vmem((wide, ff), BF16),
                vmem((owners, cols, ff), BF16),
                vmem((8, hrows, wide), BF16),
                vmem((nz, hrows, zblock), BF16),
                vmem((8, hrows, ff), BF16),
                vmem((8, hrows, ff), BF16),
                dma((10,)),
                dma((groups,)), dma((groups,)),
                dma((8,)), dma((8,)),
                dma((8,)), dma((8,)),
                dma((nz,)), dma((nz,)),
                dma((n,)), dma((n, 4)),
                dma((n,)), dma((n, 4)),
                dma((n,)), dma((n // 4,)),
                dma((owners,)), dma((owners,)),
                dma((8,)), dma((nz, 8 // nz)),
                dma((8,)), dma((8,)),
            ],
            compiler_params=pltpu.CompilerParams(collective_id=0, has_side_effects=True),
            name="moe_step",
        )(
            hot, own_count, help_count, jnp.swapaxes(scales, 0, 1), act_t, act_help[0],
            weight[0], dy_own[0], dy_help[0],
        )
        done = pl.pallas_call(
            finish,
            out_shape=(jax.ShapeDtypeStruct((ff, depth), BF16), *mid),
            in_specs=[smem] + [far] * 7,
            out_specs=(far,) * 6,
            scratch_shapes=[
                vmem((ff, rows), BF16), vmem((rows, depth), BF16), vmem((ff, depth), BF16),
                *(vmem(a.shape, a.dtype) for a in mid), dma((19,)),
            ],
            name="finish",
        )(own_count, act_t, dy_own[0], *outs)
        own_grad, own, dact_own, helped, dact_help, hot_grad = done
        dact_own = jnp.swapaxes(dact_own[None], 1, 2)
        return own[None], dact_own, own_grad[None], helped[None], dact_help[None], hot_grad.T

    return jax.shard_map(
        body,
        mesh=mesh,
        in_specs=(
            P("expert", "hidden", None),
            P("expert", None, None),
            P("expert", None, "hidden"),
            P("expert", None, None),
            P("expert"),
            P("expert", None, "hidden"),
            P("expert", None, None),
            P("expert"),
            P(),
        ),
        out_specs=(
            P("expert", None, "hidden"),
            P("expert", None, "hidden"),
            P("expert", "hidden", None),
            P("expert", None, "hidden"),
            P("expert", None, "hidden"),
            P("hidden", "expert"),
        ),
        check_vma=False,
    )
```

```python
import functools

import jax
import jax.numpy as jnp
from jax import lax
from jax.experimental import pallas as pl
from jax.experimental.pallas import tpu as pltpu
from jax.sharding import PartitionSpec as P

MESH = pl.DeviceIdType.MESH
BF16 = jnp.bfloat16
F32 = jnp.float32
LANES = 128
NT = (((1,), (1,)), ((), ()))
TN = (((0,), (0,)), ((), ()))


def kernel(
    cfg,
    hot_h, own_count_h, help_count_h, scales_h, act_own_h, act_help_h, weight, dy_own, dy_help,
    y_own, dact_own, y_help, dact_help, hot_grad,
    hot, own_count, help_count, scales, ao_v, ah_v,
    w_v, dyo_v, deq, own_a, a8, g8, mine, give, got, r1, s2, r2, wb,
    yp, ry, dw, rd, ys, ryh, da_give, da_got,
    load_sem, ex_s, ex_r, xa_s, xa_r, xg_s, xg_r, z_s, z_r,
    s1_s, s1_r, s2_s, s2_r, s4_s, s4_r, dw_s, dw_r, yh_s, yh_r, da_s, da_r,
):
    n, nz, ff, rows, hrows, depth = cfg
    half = depth // 2
    zblock = depth // nz
    wide = depth // 8
    spread = 8 // nz
    owners = 2 * n * n // 8
    cols = wide // owners
    parts = 4
    tall = ff // 2
    e, z = lax.axis_index("expert"), lax.axis_index("hidden")
    x, y, c = lax.div(e, 2 * n), lax.rem(lax.div(e, 2), n), lax.rem(e, 2)
    o = 1 - c

    def at(px, py, pc, pz):
        return ((px * n + py) * 2 + pc, pz)

    first = o * x + c * y
    second = o * y + c * x
    first_p = o * y + c * x

    def along_first(p):
        return at(o * p + c * x, o * y + c * p, c, z)

    def along_second(p):
        return at(o * x + c * p, o * p + c * y, c, z)

    def mate(j, pz):
        return at(
            x - lax.rem(x, 2) + lax.rem(lax.div(j, 2), 2), y - lax.rem(y, 2) + lax.rem(j, 2),
            lax.div(j, 4), pz,
        )

    def block_of(j):
        jc, jx, jy = lax.div(j, 4), lax.rem(lax.div(j, 2), 2), lax.rem(j, 2)
        return 4 * jc + (1 - jc) * (2 * jx + jy) + jc * (2 * jy + jx)

    me = 4 * c + 2 * lax.rem(x, 2) + lax.rem(y, 2)
    mb = block_of(me)

    def holder(b, i):
        f = 2 * lax.div(i, n // 2) + lax.rem(lax.div(b, 2), 2)
        s = 2 * lax.rem(i, n // 2) + lax.rem(b, 2)
        bc = lax.div(b, 4)
        return at((1 - bc) * f + bc * s, (1 - bc) * s + bc * f, bc, z)

    seat = lax.div(first, 2) * (n // 2) + lax.div(second, 2)

    partner = at(x, y, o, z)

    def loop(low, high, body):
        def step(i, carry):
            body(i)
            return carry

        lax.fori_loop(low, high, step, 0)

    def nth(i, count):
        turn = jnp.where(lax.rem(i, 2) == 0, lax.div(i, 2) + 1, count - lax.div(i + 1, 2))
        return jnp.where(i == count - 1, 0, turn)

    def remote(src, dst, send, recv, device):
        return pltpu.make_async_remote_copy(
            src_ref=src, dst_ref=dst, send_sem=send, recv_sem=recv,
            device_id=device, device_id_type=MESH,
        )

    col_p = pl.multiple_of(o * half, half)
    col_m = pl.multiple_of(c * half, half)
    col_b = pl.multiple_of(mb * wide, wide)

    def local(src, dst, sem):
        return pltpu.make_async_copy(src, dst, load_sem.at[sem])

    load_ah = local(act_help_h, ah_v, 0)
    load_hc = local(help_count_h, help_count, 1)
    load_hot = local(hot_h, hot, 2)
    load_sc = local(scales_h, scales, 3)
    load_wp = local(weight.at[:, pl.ds(col_p, half)], w_v.at[:, pl.ds(col_p, half)], 4)
    load_wm = local(weight.at[:, pl.ds(col_m, half)], w_v.at[:, pl.ds(col_m, half)], 5)
    load_ao = local(act_own_h, ao_v, 6)
    load_oc = local(own_count_h, own_count, 7)
    load_g = local(dy_help.at[:, pl.ds(col_b, wide)], g8.at[me], 8)
    load_dyo = local(dy_own, dyo_v, 9)
    for load in (load_ah, load_hc, load_hot, load_sc, load_wp, load_wm):
        load.start()
    for load in (load_g, load_ao, load_oc, load_dyo):
        load.start()

    barrier = pltpu.get_barrier_semaphore()

    def greet(device):
        pl.semaphore_signal(barrier, inc=1, device_id=device, device_id_type=MESH)

    def greet_lines(d):
        greet(along_first(lax.rem(first + d, n)))
        greet(along_second(lax.rem(second + d, n)))

    def greet_z(d):
        greet(at(x, y, c, lax.rem(z + d, nz)))

    def greet_mate(d):
        greet(mate(lax.rem(me + d, 8), z))

    my_b = lax.div(e, owners)
    in_b = (mb == my_b).astype(jnp.int32)

    def sender(i):
        b = z * spread + lax.rem(i, spread)
        bc = lax.div(b, 4)
        b1, b0 = lax.rem(lax.div(b, 2), 2), lax.rem(b, 2)
        return 4 * bc + (1 - bc) * (2 * b1 + b0) + bc * (2 * b0 + b1), lax.div(i, spread)

    loop(1, n, greet_lines)
    loop(1, nz, greet_z)
    loop(1, 8, greet_mate)

    load_ah.wait()
    load_hc.wait()
    live_help = lax.broadcasted_iota(jnp.int32, (hrows, ff), 0) < help_count[0]
    help_a = jnp.where(live_help, ah_v[...].astype(F32), 0.0).astype(BF16)
    a8[me] = help_a

    load_hot.wait()
    load_sc.wait()
    flag = jnp.where(hot[0] == e, 1.0, 0.0).astype(F32)

    def tile_of(base, t):
        b = 2 * lax.rem(t, 2) + lax.rem(lax.div(t, 2), 2)
        return base + b * (wide // LANES) + 2 * lax.div(t, 4)

    third = ff // 3
    runs = (
        ((0, third, 0), (third, tall - third, 1)),
        ((tall, 2 * third - tall, 1), (2 * third, third, 2)),
    )

    def scaled(h, col_base, at_first, dest):
        def one(i):
            t = lax.rem(at_first + nth(i, n), n)
            tile = tile_of(lax.div(col_base, LANES), t) + h // 2
            col = pl.multiple_of(tile * LANES, LANES)
            for start, size, part in runs[h % 2]:
                span = pl.ds(start, size)
                scale = scales[lax.div(3 * z + part, 2), 0, tile]
                wide = w_v[span, pl.ds(col, LANES)].astype(F32) * scale
                deq[span, pl.ds(col, LANES)] = wide.astype(BF16)
                dest[i, h // 2, span, :] = (wide * flag).astype(BF16)

        loop(0, n, one)

    pl.semaphore_wait(barrier, 2 * (n - 1) + (nz - 1) + 7)

    def send_mate(d):
        j = lax.rem(me + d, 8)
        remote(a8.at[me], a8.at[me], xa_s.at[j], xa_r.at[me], mate(j, z)).start()
        block = pl.ds(pl.multiple_of(block_of(j) * wide, wide), wide)
        remote(dy_help.at[:, block], g8.at[me], xg_s.at[j], xg_r.at[me], mate(j, z)).start()

    loop(1, 8, send_mate)

    load_wp.wait()

    def exchange(h):
        there = (slice(None), h // 2, pl.ds((h % 2) * tall, tall))
        return remote(give.at[there], got.at[there], ex_s.at[h], ex_r.at[h], partner)

    for h in range(parts):
        scaled(h, col_p, first_p, give)
        exchange(h).start()
    load_wm.wait()

    def strip(h):
        return lax.div(h, 2), pl.ds(pl.multiple_of(lax.rem(h, 2) * tall, 16), tall)

    for h in range(parts):
        scaled(h, col_m, first, mine)
        exchange(h).wait_recv()
        k, span = h // 2, pl.ds((h % 2) * tall, tall)

        def send_first(i):
            t = lax.rem(first + nth(i, n), n)
            mine[i, k, span, :] = mine[i, k, span, :] + got[i, k, span, :]
            remote(
                mine.at[i, k, span], r1.at[first, k, span], s1_s.at[t], s1_r.at[first, h],
                along_first(t),
            ).start()

        loop(0, n - 1, send_first)
        r1[first, k, span, :] = mine[n - 1, k, span, :] + got[n - 1, k, span, :]

    load_ao.wait()
    load_oc.wait()
    live_own = lax.broadcasted_iota(jnp.int32, (ff, rows), 1) < own_count[0]
    own_a[...] = jnp.where(live_own, ao_v[...].astype(F32), 0.0).T.astype(BF16)

    def own_partial(pz):
        block = pl.ds(pl.multiple_of(pz * zblock, zblock), zblock)
        return jnp.dot(own_a[...], deq[:, block], preferred_element_type=F32).astype(BF16)

    def send_z(i):
        pz = lax.rem(z + nth(i, nz), nz)
        yp[pz] = own_partial(pz)
        remote(yp.at[pz], ry.at[z], z_s.at[pz], z_r.at[z], at(x, y, c, pz)).start()

    loop(0, nz - 1, send_z)
    ry[z] = own_partial(z)

    load_dyo.wait()
    kblock = 512

    def dact_step(j, total):
        block = pl.ds(pl.multiple_of(j * kblock, kblock), kblock)
        return total + lax.dot_general(
            deq[:, block], dyo_v[:, block], NT, preferred_element_type=F32
        )

    total = lax.fori_loop(0, depth // kblock, dact_step, jnp.zeros((ff, rows), F32))
    dact_own[...] = jnp.where(live_own, total, 0.0).astype(BF16)

    parity = lax.rem(lax.div(first, 2), 2)
    keeps = parity == lax.rem(second, 2)
    u = lax.div(first, 4)

    def reduce_part(h):
        k, span = strip(h)

        def wait_first(d):
            p = lax.rem(first + d, n)
            there = r1.at[p, k, span]
            remote(there, there, s1_s.at[p], s1_r.at[p, h], along_first(p)).wait_recv()

        loop(1, n, wait_first)
        piece = r1[0, k, span, :].astype(F32)
        for p in range(1, n):
            piece = piece + r1[p, k, span, :].astype(F32)
        s2[k, span, :] = piece.astype(BF16)

        def send_second(i):
            p = lax.rem(2 * i + second - lax.rem(second, 2) + parity, n)

            @pl.when(p != second)
            def _():
                remote(
                    s2.at[k, span], r2.at[second, k, span], s2_s.at[p], s2_r.at[second, h],
                    along_second(p),
                ).start()

        loop(0, n // 2, send_second)

        @pl.when(keeps)
        def _():
            r2[second, k, span, :] = piece.astype(BF16)

    def keep_part(h):
        k, span = strip(h)

        def wait_second(d):
            p = lax.rem(second + d, n)
            there = r2.at[p, k, span]
            remote(there, there, s2_s.at[p], s2_r.at[p, h], along_second(p)).wait_recv()

        loop(1, n, wait_second)
        piece = r2[0, k, span, :].astype(F32)
        for p in range(1, n):
            piece = piece + r2[p, k, span, :].astype(F32)
        there = wb.at[u, k, span]
        there[...] = piece.astype(BF16)

        def send_last(i):
            p = lax.rem(first + 2 * i, n)
            remote(there, there, s4_s.at[p], s4_r.at[u], along_first(p)).start()

        loop(1, n // 2, send_last)

    def stage(i):
        pl.when(i < parts)(lambda: reduce_part(i))
        pl.when((i >= 2) & keeps)(lambda: keep_part(i - 2))

    loop(0, parts, stage)

    loop(parts, parts + 2, stage)

    load_g.wait()

    def wait_mate(d):
        j = lax.rem(me + d, 8)
        remote(a8.at[j], a8.at[j], xa_s.at[j], xa_r.at[j], mate(j, z)).wait_recv()
        remote(g8.at[j], g8.at[j], xg_s.at[j], xg_r.at[j], mate(j, z)).wait_recv()

    loop(1, 8, wait_mate)
    dw[...] = lax.dot_general(
        g8[...].reshape(8 * hrows, wide), a8[...].reshape(8 * hrows, ff), TN,
        preferred_element_type=F32,
    ).astype(BF16)

    def each_owner(body):
        def one(d):
            i = lax.rem(seat + d, owners)
            part = dw.at[pl.ds(pl.multiple_of(i * cols, cols), cols)]
            owner = mb * owners + i
            copy = remote(part, rd.at[seat], dw_s.at[i], dw_r.at[seat], (owner, z))
            body(copy, part, owner == e)

        loop(0, owners, one)

    def send_dw(copy, part, own):
        pl.when(jnp.logical_not(own))(copy.start)

        @pl.when(own)
        def _():
            rd[seat] = part[...]

    each_owner(send_dw)

    def wait_z(d):
        p = lax.rem(z + d, nz)
        remote(ry.at[p], ry.at[p], z_s.at[p], z_r.at[p], at(x, y, c, p)).wait_recv()

    loop(1, nz, wait_z)

    def sum_z(i):
        span = pl.ds(pl.multiple_of(i * 16, 16), 16)
        piece = ry[0, span, :].astype(F32)
        for p in range(1, nz):
            piece = piece + ry[p, span, :].astype(F32)
        y_own[span, :] = piece.astype(BF16)

    loop(0, rows // 16, sum_z)

    for i in range(n // 4):
        t = lax.rem(first, 2) + 2 * lax.rem(second, 2) + 4 * i

        @pl.when(t != first)
        def _():
            remote(wb.at[i], wb.at[i], s4_s.at[t], s4_r.at[i], along_first(t)).wait_recv()

    block = jnp.concatenate([wb[j // 2, j % 2] for j in range(n // 2)], axis=1)
    out = jnp.dot(a8[...].reshape(8 * hrows, ff), block, preferred_element_type=F32)
    ys[...] = out.astype(BF16).reshape(8, hrows, wide)
    pz = lax.div(mb, spread)
    sub = lax.rem(mb, spread)
    landing = pl.ds(pl.multiple_of(sub * wide, wide), wide)

    def helped(j):
        return remote(
            ys.at[j], ryh.at[z, :, landing], yh_s.at[j], yh_r.at[z, sub], mate(j, pz)
        )

    def send_helped(d):
        j = lax.rem(me + d, 8)
        own = (j == me) & (pz == z)
        pl.when(jnp.logical_not(own))(helped(j).start)

        @pl.when(own)
        def _():
            ryh[z, :, landing] = ys[j]

    loop(0, 8, send_helped)
    da = lax.dot_general(
        g8[...].reshape(8 * hrows, wide), block, NT, preferred_element_type=F32
    )
    da_give[...] = da.astype(BF16).reshape(8, hrows, ff)

    def da_copy(j):
        return remote(da_give.at[j], da_got.at[me], da_s.at[j], da_r.at[me], mate(j, z))

    loop(1, 8, lambda d: da_copy(lax.rem(me + d, 8)).start())
    da_got[me] = da_give[me]

    def wait_dw(i):
        @pl.when((i != seat) | (in_b == 0))
        def _():
            remote(rd.at[i], rd.at[i], dw_s.at[i], dw_r.at[i], holder(my_b, i)).wait_recv()

    loop(0, owners, wait_dw)
    total = rd[0].astype(F32)
    for p in range(1, owners):
        total = total + rd[p].astype(F32)
    hot_grad[...] = total

    def wait_da(d):
        j = lax.rem(me + d, 8)
        remote(da_got.at[j], da_got.at[j], da_s.at[j], da_r.at[j], mate(j, z)).wait_recv()

    loop(1, 8, wait_da)
    total = da_got[0].astype(F32)
    for j in range(1, 8):
        total = total + da_got[j].astype(F32)
    dact_help[...] = jnp.where(live_help, total, 0.0).astype(BF16)

    def wait_helped(i):
        j, p = sender(i)

        @pl.when((j != me) | (p != z))
        def _():
            s = lax.rem(i, spread)
            there = ryh.at[p, :, pl.ds(pl.multiple_of(s * wide, wide), wide)]
            remote(there, there, yh_s.at[0], yh_r.at[p, s], mate(j, p)).wait_recv()

    loop(0, 8, wait_helped)
    piece = ryh[0].astype(F32)
    for p in range(1, nz):
        piece = piece + ryh[p].astype(F32)
    y_help[...] = piece.astype(BF16)

    for h in range(parts):
        exchange(h).wait_send()

    def drain_mate(d):
        j = lax.rem(me + d, 8)
        remote(a8.at[j], a8.at[j], xa_s.at[j], xa_r.at[j], mate(j, z)).wait_send()
        remote(g8.at[j], g8.at[j], xg_s.at[j], xg_r.at[j], mate(j, z)).wait_send()
        da_copy(j).wait_send()

    loop(1, 8, drain_mate)

    def drain_first(d):
        p = lax.rem(first + d, n)
        remote(r1.at[p], r1.at[p], s1_s.at[p], s1_r.at[p, 0], along_first(p)).wait_send()

    loop(1, n, drain_first)

    def drain_second(i):
        p = lax.rem(2 * i + second - lax.rem(second, 2) + parity, n)

        @pl.when(p != second)
        def _():
            remote(r2.at[p], r2.at[p], s2_s.at[p], s2_r.at[p, 0], along_second(p)).wait_send()

        @pl.when(keeps & (i > 0))
        def _():
            p = lax.rem(first + 2 * i, n)
            remote(wb.at[u], wb.at[u], s4_s.at[p], s4_r.at[u], along_first(p)).wait_send()

    loop(0, n // 2, drain_second)
    each_owner(lambda copy, part, own: pl.when(jnp.logical_not(own))(copy.wait_send))

    def drain_line(d):
        p = lax.rem(z + d, nz)
        remote(ry.at[p], ry.at[p], z_s.at[p], z_r.at[p], at(x, y, c, p)).wait_send()

    loop(1, nz, drain_line)

    def drain_helped(j):
        pl.when((j != me) | (pz != z))(helped(j).wait_send)

    loop(0, 8, drain_helped)


def finish(*refs):
    own_count, act, dy = refs[:3]
    mids, grad, outs = refs[3:8], refs[8], refs[9:14]
    act_v, dy_v, grad_v, held, sem = refs[14], refs[15], refs[16], refs[17:22], refs[22]
    steps = 4
    width = dy.shape[1] // steps

    def part(ref, j):
        return ref.at[:, pl.ds(j * width, width)]

    def copy(src, dst, i):
        return pltpu.make_async_copy(src, dst, sem.at[i])

    loads = [copy(act, act_v, 0)]
    loads += [copy(part(dy, j), part(dy_v, j), 1 + j) for j in range(steps)]
    takes = [copy(mids[i], held[i], 1 + steps + i) for i in range(5)]
    gives = [copy(held[i], outs[i], 6 + steps + i) for i in range(5)]
    stores = [copy(part(grad_v, j), part(grad, j), 11 + steps + j) for j in range(steps)]
    for load in loads + takes:
        load.start()
    loads[0].wait()
    live = lax.broadcasted_iota(jnp.int32, act.shape, 1) < own_count[0]
    rows = jnp.where(live, act_v[...].astype(F32), 0.0).astype(BF16)
    for j in range(steps):
        loads[1 + j].wait()
        span = pl.ds(j * width, width)
        grad_v[:, span] = jnp.dot(
            rows, dy_v[:, span], preferred_element_type=F32
        ).astype(BF16)
        stores[j].start()
    for take, give in zip(takes, gives):
        take.wait()
        give.start()
    for out in gives + stores:
        out.wait()


def solution(mesh):
    nz = mesh.shape["hidden"]
    n = 1
    while 2 * n * n < mesh.shape["expert"]:
        n += 1

    def body(weight, scales, act_own, dy_own, own_count, act_help, dy_help, help_count, hot):
        ff, depth = weight.shape[1:]
        rows, hrows = act_own.shape[1], act_help.shape[1]
        half, zblock, wide = depth // 2, depth // nz, depth // 8
        owners, cols = n * n // 4, depth // (2 * n * n)
        vmem = pltpu.VMEM
        dma = pltpu.SemaphoreType.DMA
        smem = pl.BlockSpec(memory_space=pltpu.SMEM)
        near = pl.BlockSpec(memory_space=pltpu.VMEM)
        far = pl.BlockSpec(memory_space=pl.ANY)
        act_t = jnp.swapaxes(act_own, 1, 2)[0]
        mid = (
            jax.ShapeDtypeStruct((rows, zblock), BF16),
            jax.ShapeDtypeStruct((ff, rows), BF16),
            jax.ShapeDtypeStruct((hrows, zblock), BF16),
            jax.ShapeDtypeStruct((hrows, ff), BF16),
            jax.ShapeDtypeStruct((cols, ff), F32),
        )
        outs = pl.pallas_call(
            functools.partial(kernel, (n, nz, ff, rows, hrows, depth)),
            out_shape=mid,
            in_specs=[pl.BlockSpec(memory_space=pltpu.HBM)] * 4 + [far] * 5,
            out_specs=(near,) * 5,
            scratch_shapes=[
                pltpu.SMEM((1,), jnp.int32),
                pltpu.SMEM((1,), jnp.int32),
                pltpu.SMEM((1,), jnp.int32),
                pltpu.SMEM((scales.shape[1], 1, scales.shape[2]), F32),
                vmem((ff, rows), BF16),
                vmem((hrows, ff), BF16),
                vmem((ff, depth), BF16),
                vmem((rows, depth), BF16),
                vmem((ff, depth), BF16),
                vmem((rows, ff), BF16),
                vmem((8, hrows, ff), BF16),
                vmem((8, hrows, wide), BF16),
                vmem((n, 2, ff, LANES), BF16),
                vmem((n, 2, ff, LANES), BF16),
                vmem((n, 2, ff, LANES), BF16),
                vmem((n, 2, ff, LANES), BF16),
                vmem((2, ff, LANES), BF16),
                vmem((n, 2, ff, LANES), BF16),
                vmem((n // 4, 2, ff, LANES), BF16),
                vmem((nz, rows, zblock), BF16),
                vmem((nz, rows, zblock), BF16),
                vmem((wide, ff), BF16),
                vmem((owners, cols, ff), BF16),
                vmem((8, hrows, wide), BF16),
                vmem((nz, hrows, zblock), BF16),
                vmem((8, hrows, ff), BF16),
                vmem((8, hrows, ff), BF16),
                dma((10,)),
                dma((4,)), dma((4,)),
                dma((8,)), dma((8,)),
                dma((8,)), dma((8,)),
                dma((nz,)), dma((nz,)),
                dma((n,)), dma((n, 4)),
                dma((n,)), dma((n, 4)),
                dma((n,)), dma((n // 4,)),
                dma((owners,)), dma((owners,)),
                dma((8,)), dma((nz, 8 // nz)),
                dma((8,)), dma((8,)),
            ],
            compiler_params=pltpu.CompilerParams(collective_id=0, has_side_effects=True),
            name="moe_step",
        )(
            hot, own_count, help_count, jnp.swapaxes(scales, 0, 1), act_t, act_help[0],
            weight[0], dy_own[0], dy_help[0],
        )
        done = pl.pallas_call(
            finish,
            out_shape=(jax.ShapeDtypeStruct((ff, depth), BF16), *mid),
            in_specs=[smem] + [far] * 7,
            out_specs=(far,) * 6,
            scratch_shapes=[
                vmem((ff, rows), BF16), vmem((rows, depth), BF16), vmem((ff, depth), BF16),
                *(vmem(a.shape, a.dtype) for a in mid), dma((19,)),
            ],
            name="finish",
        )(own_count, act_t, dy_own[0], *outs)
        own_grad, own, dact_own, helped, dact_help, hot_grad = done
        dact_own = jnp.swapaxes(dact_own[None], 1, 2)
        return own[None], dact_own, own_grad[None], helped[None], dact_help[None], hot_grad.T

    return jax.shard_map(
        body,
        mesh=mesh,
        in_specs=(
            P("expert", "hidden", None),
            P("expert", None, None),
            P("expert", None, "hidden"),
            P("expert", None, None),
            P("expert"),
            P("expert", None, "hidden"),
            P("expert", None, None),
            P("expert"),
            P(),
        ),
        out_specs=(
            P("expert", None, "hidden"),
            P("expert", None, "hidden"),
            P("expert", "hidden", None),
            P("expert", None, "hidden"),
            P("expert", None, "hidden"),
            P("hidden", "expert"),
        ),
        check_vma=False,
    )
```
